32 devices in a mesh: seq: 16 (over z, y, core), grp: 2 (over x).
Axes of the slice: x: 2, y: 2, z: 4, core: 2. Of those that a mesh axis runs over, the one named last changes fastest.
Arguments:
- units: bfloat16 [4096, 1024], P(('grp', 'seq')), parts along dimension 0, may hold values from -6 to 6
- durations: int32 [4096], P(('grp', 'seq')), parts along dimension 0, may hold values from 1 to 12, 12288 in all
- seg_ids: int32 [4096], P(('grp', 'seq')), parts along dimension 0, may hold values from 0 to 7, never falling along the last dimension, each value on 1 to 1024 neighbouring positions
- ln_gain: float32 [1024], replicated, may hold values from 0.1 to 1.9
- w_qkv: bfloat16 [1024, 3072], replicated, may hold values from -8 to 8
- w_out: bfloat16 [1024, 1024], replicated, may hold values from -0.1875 to 0.1875
- w_proj: bfloat16 [1024, 512], replicated, may hold values from -0.1875 to 0.1875
- conv_w: bfloat16 [5, 512, 512], replicated, may hold values from -0.125 to 0.125
- conv_b: float32 [512], replicated, may hold values from -3 to 3
- conv_gain: float32 [512], replicated, may hold values from 0.1 to 1.9
Outputs:
- frames_out: bfloat16 [24576, 512], P(('grp', 'seq')), parts along dimension 0
The draws below stay inside these ranges and needn't reach their ends.
There are 2 independent parts, one for each index of `grp`. The reference program is written for one: setup_inputs(seed, part) draws one part's arguments, and reference() takes and returns one part's arrays. A program takes and returns all parts, laid end to end along the dimension named above; an argument that names none is the same for every part. Nothing has to cross between parts.
All inputs are finite; a program needn't handle non-finite values. No bound on the sum of `durations` on one device may be relied on, other than what follows from the above.
Results may differ from the reference program's by a relative error of at most 0.0098.
Values may be sent and summed in bfloat16 or wider, within the bound.
No kernel may reach another device: no remote copies, remote signals or barrier semaphores. Data moves between devices by JAX's collectives and lax.ppermute only.
A program may use at most 128 MiB of HBM per device.

```python
import math
import jax
import jax.numpy as jnp
import numpy as np
from jax import lax

D = 1024
HEADS = 16
C = 512
KERNEL = 5
SEGS = 8
UNITS = 2048
FRAMES = 12288


def draw_units(key, part):
    base = jax.random.truncated_normal(key, -6.0, 6.0, (UNITS, D), jnp.float32)
    return base.astype(jnp.bfloat16)


def draw_w_qkv(key, part):
    matrix = jax.random.truncated_normal(key, -6.0, 6.0, (D, 3 * D), jnp.float32) / math.sqrt(D)
    query_part = 3.0 * matrix[:, :D]
    key_part = 1.5 * matrix[:, D:2 * D]
    return jnp.concatenate([query_part, key_part, matrix[:, 2 * D:]], axis=1).astype(jnp.bfloat16)


def length_profile(number_of, total, reach, slope):
    weights = [(1 << 20) // math.isqrt(rank ** slope) + 1 for rank in range(2, number_of + 1)]
    surplus, counts = total - reach - (number_of - 1), [1] * (number_of - 1)
    while surplus > 0:
        free = [i for i in range(number_of - 1) if counts[i] < reach]
        mass, remaining = sum([weights[i] for i in free]), surplus
        for i in free:
            addition = min(reach - counts[i], max(1, remaining * weights[i] // mass), surplus)
            counts[i] = counts[i] + addition
            surplus = surplus - addition
    return np.array([reach] + counts)


def ragged_sizes(own_key, number_of, total, reach, skew):
    if number_of == 2:
        one = jax.random.randint(own_key, (), max(1, total - reach), min(reach, total - 1) + 1)
        return jnp.stack([one, total - one])
    lengths = jnp.asarray(length_profile(number_of, total, reach, skew), jnp.int32)
    pairs = (number_of - 1) // 2
    giver, taker = lengths[1:1 + 2 * pairs:2], lengths[2:2 + 2 * pairs:2]
    margin = jnp.minimum(giver - 1, reach - taker)
    shifted = jax.random.randint(jax.random.fold_in(own_key, 1), (pairs,), 0, 1 << 20) % (margin + 1)
    lengths = lengths.at[1:1 + 2 * pairs:2].set(giver - shifted).at[2:2 + 2 * pairs:2].set(taker + shifted)
    return lengths[jax.random.permutation(jax.random.fold_in(own_key, 2), number_of)]


def gaussian(stream_key, extent, width, bound, kind=jnp.bfloat16):
    values = width * jax.random.normal(stream_key, extent, jnp.float32)
    return jnp.clip(values, min=-bound, max=bound).astype(kind)


def setup_inputs(seed: int = 0, part: int = 0) -> dict:
    seeds = jax.random.split(jax.random.key(seed), 11)
    part_keys = jax.random.split(jax.random.fold_in(seeds[10], part), 11)
    units = draw_units(jax.random.fold_in(jax.random.fold_in(seeds[10], part), 71), part)
    durations = ragged_sizes(part_keys[1], UNITS, FRAMES, 12, 2).astype(jnp.int32)
    seg_ids = jnp.searchsorted(jnp.cumsum(ragged_sizes(part_keys[2], SEGS, UNITS, UNITS // 2, 0)), jnp.arange(UNITS), side="right").astype(jnp.int32)
    ln_gain = jnp.clip(1.0 + 0.18 * jax.random.normal(seeds[3], (D,), jnp.float32), 0.1, 1.9)
    w_qkv = draw_w_qkv(jax.random.fold_in(seeds[10], 71), part)
    w_out = gaussian(seeds[5], (D, D), D ** -0.5, 0.1875)
    w_proj = gaussian(seeds[6], (D, C), D ** -0.5, 0.1875)
    conv_w = gaussian(seeds[7], (KERNEL, C, C), (KERNEL * C) ** -0.5, 0.125)
    conv_b = gaussian(seeds[8], (C,), 0.5, 3.0, jnp.float32)
    conv_gain = jnp.clip(1.0 + 0.18 * jax.random.normal(seeds[9], (C,), jnp.float32), 0.1, 1.9)
    return {"units": units, "durations": durations, "seg_ids": seg_ids, "ln_gain": ln_gain, "w_qkv": w_qkv, "w_out": w_out, "w_proj": w_proj, "conv_w": conv_w, "conv_b": conv_b, "conv_gain": conv_gain}


def normalize(values, gain):
    mean = lax.optimization_barrier(jnp.mean(values, axis=-1, keepdims=True))
    centred = values - mean
    variance = lax.optimization_barrier(jnp.mean(centred * centred, axis=-1, keepdims=True))
    return centred / jnp.sqrt(variance + 1e-05) * gain

def reference(units, durations, seg_ids, ln_gain, w_qkv, w_out, w_proj, conv_w, conv_b, conv_gain):
    head_size = D // HEADS
    x = units.astype(jnp.float32)
    h = normalize(x, ln_gain).astype(jnp.bfloat16)
    qkv = jnp.dot(h, w_qkv, preferred_element_type=jnp.float32).astype(jnp.bfloat16)
    query = qkv[:, :D].reshape(UNITS, HEADS, head_size).transpose(1, 0, 2)
    keys = qkv[:, D:2 * D].reshape(UNITS, HEADS, head_size).transpose(1, 0, 2)
    values = qkv[:, 2 * D:].reshape(UNITS, HEADS, head_size).transpose(1, 0, 2)
    allowed = seg_ids[:, None] == seg_ids[None, :]
    scale = 1.0 / jnp.sqrt(jnp.float32(head_size))

    def one_head(parts):
        q_head, k_head, v_head = parts
        scores = jnp.dot(q_head, k_head.T, preferred_element_type=jnp.float32) * scale
        scores = jnp.where(allowed, scores, jnp.float32(-1e+30))
        top = lax.optimization_barrier(jnp.max(scores, axis=1, keepdims=True))
        expo = jnp.where(allowed, jnp.exp(scores - top), jnp.float32(0.0))
        total = lax.optimization_barrier(jnp.sum(expo, axis=1, keepdims=True))
        summed = jnp.dot(expo.astype(jnp.bfloat16), v_head, preferred_element_type=jnp.float32)
        return summed / total
    heads_out = lax.map(one_head, (query, keys, values))
    attended = heads_out.transpose(1, 0, 2).reshape(UNITS, D).astype(jnp.bfloat16)
    mixed = (jnp.dot(attended, w_out, preferred_element_type=jnp.float32) + x).astype(jnp.bfloat16)
    reduced = jnp.dot(mixed, w_proj, preferred_element_type=jnp.float32).astype(jnp.bfloat16)
    ends = jnp.cumsum(durations).astype(jnp.int32)
    frame_pos = jnp.arange(FRAMES, dtype=jnp.int32)
    unit_of = jnp.searchsorted(ends, frame_pos, side='right').astype(jnp.int32)
    expanded = jnp.take(reduced, unit_of, axis=0)
    half = KERNEL // 2
    padded = jnp.pad(expanded, ((half, half), (0, 0)))
    conv = jnp.zeros((FRAMES, C), jnp.float32) + conv_b
    for tap in range(KERNEL):
        conv = conv + jnp.dot(padded[tap:tap + FRAMES], conv_w[tap], preferred_element_type=jnp.float32)
    result = expanded.astype(jnp.float32) + normalize(jax.nn.relu(conv), conv_gain)
    return result.astype(jnp.bfloat16)
```

```python
import functools
import math

import jax
import jax.numpy as jnp
from jax import lax
from jax.experimental import pallas as pl
from jax.experimental.pallas import tpu as pltpu
from jax.sharding import PartitionSpec as P

HEADS = 16
KERNEL = 5
SEGS = 8
DUR_MEAN = 6
EPS = 1e-05

WIN = 160
ALIGN = 8
LANES = 256
KEYS = 256
HALO = 8
LOW = -1e30
MASKED = -2e30


def rows_normalized(values, gain):
    mean = jnp.mean(values, axis=-1, keepdims=True)
    centred = values - mean
    variance = jnp.mean(centred * centred, axis=-1, keepdims=True)
    return centred * lax.rsqrt(variance + EPS) * gain


def project_body(first, sc, x0, x1, x2, x3, gain, w, *rest):
    if first:
        kv, xa, xs, hs, sems = rest
    else:
        _, _, kv, xa, xs, hs, sems = rest
    rows = x0.shape[0]

    @pl.when(pl.program_id(0) == 0)
    def _():
        copies = []
        for i, ref in enumerate((x0, x1, x2, x3)):
            block = (sc[1] ^ (i // 2)) * 2 + (sc[2] ^ (i % 2))
            start = pl.multiple_of(block * rows, rows)
            copies.append(pltpu.make_async_copy(ref, xs.at[pl.ds(start, rows)], sems.at[i]))
        for copy in copies:
            copy.start()
        for copy in copies:
            copy.wait()
        for i in range(4):
            part = pl.ds(i * rows, rows)
            x = xs[part, :]
            xa[part, :] = x
            hs[part, :] = rows_normalized(x.astype(jnp.float32), gain[...]).astype(jnp.bfloat16)

    kv[...] = jnp.dot(hs[...], w[...], preferred_element_type=jnp.float32).astype(jnp.bfloat16)


def project(sc, blocks, gain, w_qkv, previous, units):
    rows, width = blocks[0].shape
    plane = 4 * rows
    cols = 512
    steps = 2 * width // cols
    first = previous is None
    any_spec = pl.BlockSpec(memory_space=pl.ANY)
    in_specs = [any_spec] * 4 + [
        pl.BlockSpec((1, width), lambda j, s: (0, 0)),
        pl.BlockSpec((width, cols), lambda j, s: (0, width // cols + j)),
    ]
    operands = [sc, *blocks, gain, w_qkv]
    aliases = {}
    if not first:
        in_specs += [any_spec] * 2
        aliases = {len(operands): 0, len(operands) + 1: 1}
        operands += list(previous)
    return pl.pallas_call(
        functools.partial(project_body, first),
        out_shape=(
            jax.ShapeDtypeStruct((units, 2 * width), jnp.bfloat16),
            jax.ShapeDtypeStruct((units, width), jnp.bfloat16),
        ),
        grid_spec=pltpu.PrefetchScalarGridSpec(
            num_scalar_prefetch=1,
            grid=(steps,),
            in_specs=in_specs,
            out_specs=(
                pl.BlockSpec((plane, cols), lambda j, s: (s[0], j)),
                pl.BlockSpec((plane, width), lambda j, s: (s[0], 0)),
            ),
            scratch_shapes=[
                pltpu.VMEM((plane, width), jnp.bfloat16),
                pltpu.VMEM((plane, width), jnp.bfloat16),
                pltpu.SemaphoreType.DMA((4,)),
            ],
        ),
        input_output_aliases=aliases,
        cost_estimate=pl.CostEstimate(
            flops=2 * plane * width * 2 * width,
            bytes_accessed=2 * (width * 2 * width + 4 * plane * width),
            transcendentals=0,
        ),
        compiler_params=pltpu.CompilerParams(vmem_limit_bytes=24 << 20),
    )(*operands)


def frames_body(
    sc, spans, gain, conv_b, conv_gain, xa, kv, w_qkv, w_out, w_proj, conv_w,
    out, wq, wo, wp, cw, keys, xw, qz, acc, tops, totals, red, expanded, sems, key_sems,
):
    width = w_out.shape[0]
    channels = w_proj.shape[1]
    head = width // HEADS
    pair = 2 * head
    frames = out.shape[0]
    half = KERNEL // 2
    scale = math.log2(math.e) / math.sqrt(head)

    load_q = pltpu.make_async_copy(w_qkv.at[:, pl.ds(0, width)], wq, sems.at[0])
    load_o = pltpu.make_async_copy(w_out, wo, sems.at[1])
    load_p = pltpu.make_async_copy(w_proj, wp, sems.at[2])
    load_c = pltpu.make_async_copy(conv_w, cw, sems.at[3])
    load_q.start()

    base, windows, frame0 = sc[0], sc[1], sc[2]

    def seg_start(v):
        return sc[4 + v]

    def window(w, carry):
        r0 = pl.multiple_of(base + w * WIN, ALIGN)
        load_x = pltpu.make_async_copy(xa.at[pl.ds(r0, WIN)], xw, sems.at[4])
        load_x.start()
        lo, hi = jnp.int32(0), jnp.int32(0)
        for v in range(SEGS):
            lo = jnp.where(r0 >= seg_start(v), seg_start(v), lo)
            hi = jnp.where(r0 + WIN - 1 >= seg_start(v), seg_start(v + 1), hi)
        t0 = lax.div(lo, KEYS)
        t1 = lax.div(hi + KEYS - 1, KEYS)

        def key_copy(t):
            part = pl.ds(pl.multiple_of(t * KEYS, KEYS), KEYS)
            return pltpu.make_async_copy(kv.at[part], keys.at[part], key_sems.at[t])

        def start_keys(t, c):
            key_copy(t).start()
            return c

        lax.fori_loop(t0, t1, start_keys, 0)

        @pl.when(w == 0)
        def _():
            load_o.start()
            load_p.start()
            load_c.start()
            load_q.wait()

        load_x.wait()
        h = rows_normalized(xw[...].astype(jnp.float32), gain[...]).astype(jnp.bfloat16)
        q = jnp.dot(h, wq[...], preferred_element_type=jnp.float32).astype(jnp.bfloat16)
        low_half = lax.broadcasted_iota(jnp.int32, (WIN, pair), 1) < head
        zero = jnp.zeros((WIN, pair), jnp.bfloat16)
        for p in range(HEADS // 2):
            part = q[:, p * pair : (p + 1) * pair]
            qz[2 * p] = jnp.where(low_half, part, zero)
            qz[2 * p + 1] = jnp.where(low_half, zero, part)
        acc[...] = jnp.zeros_like(acc)
        tops[...] = jnp.full_like(tops, LOW)
        totals[...] = jnp.zeros_like(totals)

        row = r0 + lax.broadcasted_iota(jnp.int32, (WIN, KEYS), 0)
        row_lo = jnp.zeros((WIN, KEYS), jnp.int32)
        row_hi = jnp.zeros((WIN, KEYS), jnp.int32)
        for v in range(SEGS):
            row_lo = jnp.where(row >= seg_start(v), seg_start(v), row_lo)
            row_hi = jnp.where(row >= seg_start(v), seg_start(v + 1), row_hi)

        def key_step(t, c):
            key_copy(t).wait()
            k0 = pl.multiple_of(t * KEYS, KEYS)
            rows = pl.ds(k0, KEYS)
            col = k0 + lax.broadcasted_iota(jnp.int32, (WIN, KEYS), 1)
            allowed = (col >= row_lo) & (col < row_hi)
            for p in range(HEADS // 2):
                k_pair = keys[rows, p * pair : (p + 1) * pair]
                v_pair = keys[rows, width + p * pair : width + (p + 1) * pair]
                parts, alphas = [], []
                for i in range(2):
                    n = 2 * p + i
                    s = lax.dot_general(
                        qz[n], k_pair, (((1,), (1,)), ((), ())), preferred_element_type=jnp.float32
                    )
                    s = jnp.where(allowed, s * scale, MASKED)
                    top = tops[n][:, :1]
                    new_top = jnp.maximum(top, jnp.max(s, axis=1, keepdims=True))
                    expo = jnp.exp2(s - new_top)
                    alpha = jnp.exp2(top - new_top)
                    tops[n] = jnp.broadcast_to(new_top, (WIN, 128))
                    totals[n] = totals[n] * alpha + jnp.sum(expo, axis=1, keepdims=True)
                    alphas.append(alpha)
                    parts.append(
                        jnp.dot(expo.astype(jnp.bfloat16), v_pair, preferred_element_type=jnp.float32)
                    )
                cols = slice(p * pair, (p + 1) * pair)
                acc[:, cols] = acc[:, cols] * jnp.where(low_half, alphas[0], alphas[1]) + jnp.where(
                    low_half, parts[0], parts[1]
                )
            return c

        lax.fori_loop(t0, t1, key_step, 0)

        outs = []
        for p in range(HEADS // 2):
            total = jnp.where(low_half, totals[2 * p][:, :1], totals[2 * p + 1][:, :1])
            total = jnp.where(total == 0.0, 1.0, total)
            outs.append((acc[:, p * pair : (p + 1) * pair] / total).astype(jnp.bfloat16))
        attended = jnp.concatenate(outs, axis=1)

        @pl.when(w == 0)
        def _():
            load_o.wait()
            load_p.wait()

        mixed = jnp.dot(attended, wo[...], preferred_element_type=jnp.float32) + xw[...].astype(
            jnp.float32
        )
        reduced = jnp.dot(
            mixed.astype(jnp.bfloat16), wp[...], preferred_element_type=jnp.float32
        ).astype(jnp.bfloat16)
        red[pl.ds(0, WIN), :] = reduced
        red[pl.ds(WIN, LANES - WIN), :] = jnp.zeros((LANES - WIN, channels), jnp.bfloat16)
        shape = (frames + 2 * HALO, LANES)
        frame = frame0 - HALO + lax.broadcasted_iota(jnp.int32, shape, 0)
        begins = spans[pl.ds(2 * w, 1), :]
        ends = spans[pl.ds(2 * w + 1, 1), :]
        pick = jnp.where((frame >= begins) & (frame < ends), 1.0, 0.0).astype(jnp.bfloat16)
        rows = jnp.dot(pick, red[...], preferred_element_type=jnp.float32)

        @pl.when(w == 0)
        def _():
            expanded[...] = rows

        @pl.when(w > 0)
        def _():
            expanded[...] += rows

        return carry

    lax.fori_loop(0, windows, window, 0)

    load_c.wait()
    block = 256
    for b in range(frames // block):
        conv = jnp.zeros((block, channels), jnp.float32) + conv_b[...]
        for tap in range(KERNEL):
            part = expanded[pl.ds(b * block + HALO - half + tap, block), :].astype(jnp.bfloat16)
            conv = conv + jnp.dot(part, cw[tap], preferred_element_type=jnp.float32)
        result = expanded[pl.ds(b * block + HALO, block), :] + rows_normalized(
            jnp.maximum(conv, 0.0), conv_gain[...]
        )
        out[pl.ds(b * block, block), :] = result.astype(jnp.bfloat16)


def frames_call(sc, spans, gain, conv_b, conv_gain, xa, kv, w_qkv, w_out, w_proj, conv_w, frames):
    units, width = xa.shape
    channels = w_proj.shape[1]
    any_spec = pl.BlockSpec(memory_space=pl.ANY)
    vmem = pl.BlockSpec(memory_space=pltpu.VMEM)
    return pl.pallas_call(
        frames_body,
        out_shape=jax.ShapeDtypeStruct((frames, channels), jnp.bfloat16),
        in_specs=[pl.BlockSpec(memory_space=pltpu.SMEM)] + [vmem] * 4 + [any_spec] * 6,
        out_specs=vmem,
        scratch_shapes=[
            pltpu.VMEM((width, width), jnp.bfloat16),
            pltpu.VMEM((width, width), jnp.bfloat16),
            pltpu.VMEM((width, channels), jnp.bfloat16),
            pltpu.VMEM((KERNEL, channels, channels), jnp.bfloat16),
            pltpu.VMEM((units, 2 * width), jnp.bfloat16),
            pltpu.VMEM((WIN, width), jnp.bfloat16),
            pltpu.VMEM((HEADS, WIN, 2 * width // HEADS), jnp.bfloat16),
            pltpu.VMEM((WIN, width), jnp.float32),
            pltpu.VMEM((HEADS, WIN, 128), jnp.float32),
            pltpu.VMEM((HEADS, WIN, 128), jnp.float32),
            pltpu.VMEM((LANES, channels), jnp.bfloat16),
            pltpu.VMEM((frames + 2 * HALO, channels), jnp.float32),
            pltpu.SemaphoreType.DMA((5,)),
            pltpu.SemaphoreType.DMA((units // KEYS,)),
        ],
        compiler_params=pltpu.CompilerParams(vmem_limit_bytes=48 << 20),
    )(sc, spans, gain, conv_b, conv_gain, xa, kv, w_qkv, w_out, w_proj, conv_w)


def local(units, durations, seg_ids, ln_gain, w_qkv, w_out, w_proj, conv_w, conv_b, conv_gain):
    n = lax.axis_size("seq")
    outer = n // 4
    here = lax.axis_index("seq")
    own, mid, core = here // 4, (here // 2) % 2, here % 2
    count = units.shape[0]
    total = n * count
    frame_count = DUR_MEAN * count

    def place(z, y, c):
        return (z * 2 + y) * 2 + c

    def pairs(step, dy, dc):
        return [
            (place(z, y, c), place((z + step) % outer, y ^ dy, c ^ dc))
            for z in range(outer)
            for y in range(2)
            for c in range(2)
        ]

    def send(value, step, dy=0, dc=0):
        return lax.ppermute(value, "seq", pairs(step, dy, dc))

    slot = lax.broadcasted_iota(jnp.int32, (2, n, count), 1)
    info = jnp.where(slot == here, jnp.stack([durations, seg_ids])[:, None, :], 0)
    info = info + send(info, 0, 0, 1)
    info = info + send(info, 0, 1, 0)
    info = sum([send(info, s) for s in range(1, outer)], info)
    info = info.reshape(2, total)
    dur, seg = info[0], info[1]
    ends = jnp.cumsum(dur)
    frame0 = here * frame_count
    half = KERNEL // 2
    first = jnp.sum((ends <= jnp.maximum(frame0 - half, 0)).astype(jnp.int32))
    last_frame = jnp.minimum(frame0 + frame_count + half, DUR_MEAN * total) - 1
    last = jnp.sum((ends <= last_frame).astype(jnp.int32))
    base = first // ALIGN * ALIGN
    windows = (last - base + WIN) // WIN
    base = jnp.minimum(base, total - windows * WIN)
    starts_of = jnp.sum(
        (seg[None, :] < jnp.arange(SEGS + 1, dtype=jnp.int32)[:, None]).astype(jnp.int32), axis=1
    )
    sc = jnp.concatenate([jnp.stack([base, windows, frame0, last]), starts_of])
    most = -(-(frame_count + 2 * half + ALIGN) // WIN)
    padding = jnp.zeros((most * WIN,), jnp.int32)
    spans = []
    for edge in (ends - dur, ends):
        cut = lax.dynamic_slice(jnp.concatenate([edge, padding]), (base,), (most * WIN,))
        spans.append(jnp.pad(cut.reshape(most, WIN), ((0, 0), (0, LANES - WIN))))
    spans = jnp.stack(spans, axis=1).reshape(2 * most, LANES)

    gain = ln_gain[None, :]
    state = None
    block = units
    for step in range(outer):
        following = send(block, 1) if step < outer - 1 else None
        across = send(block, 0, 1, 0)
        blocks = (block, send(block, 0, 0, 1), across, send(across, 0, 0, 1))
        plane = jnp.stack([(own - step) % outer, mid, core])
        state = project(plane, blocks, gain, w_qkv, state, total)
        block = following
    kv, xa = state
    return frames_call(
        sc, spans, gain, conv_b[None, :], conv_gain[None, :], xa, kv, w_qkv, w_out, w_proj, conv_w,
        frame_count,
    )


def solution(mesh):
    split = P(("grp", "seq"))
    in_specs = (P(("grp", "seq"), None), split, split) + (P(),) * 7
    return jax.shard_map(
        local, mesh=mesh, in_specs=in_specs, out_specs=P(("grp", "seq"), None), check_vma=False
    )
```

```python
import functools
import math

import jax
import jax.numpy as jnp
from jax import lax
from jax.experimental import pallas as pl
from jax.experimental.pallas import tpu as pltpu
from jax.sharding import PartitionSpec as P

HEADS = 16
KERNEL = 5
SEGS = 8
DUR_MEAN = 6
EPS = 1e-05

MAIN = 128
REST = 32
WIN = MAIN + REST
GROUP = 4
STACK = GROUP * WIN
ALIGN = 8
LANES = 256
HALO = 8
LOW = -1e30
MASKED = -2e30
LOADS = 8
SMALL_VMEM = 4 << 20
PROJECT_VMEM = 6 << 20
FRAMES_VMEM = 24 << 20


def rows_normalized(values, gain):
    mean = jnp.mean(values, axis=-1, keepdims=True)
    centred = values - mean
    variance = jnp.mean(centred * centred, axis=-1, keepdims=True)
    return centred * lax.rsqrt(variance + EPS) * gain


def small_call(body, out_shape, *operands):
    memory = [pl.BlockSpec(memory_space=pltpu.SMEM)] + [
        pl.BlockSpec(memory_space=pltpu.VMEM) for _ in operands[1:]
    ]
    return pl.pallas_call(
        body,
        out_shape=out_shape,
        in_specs=memory,
        compiler_params=pltpu.CompilerParams(vmem_limit_bytes=SMALL_VMEM),
    )(*operands)


def place_body(here, dur, seg, out):
    slot = lax.broadcasted_iota(jnp.int32, out.shape[1:], 0)
    for i, ref in enumerate((dur, seg)):
        out[i] = jnp.where(slot == here[0], jnp.broadcast_to(ref[...], out.shape[1:]), 0)


def join_body(here, *refs):
    refs[-1][...] = sum((ref[...] for ref in refs[1:-1]), refs[0][...])


def counted(condition):
    return jnp.sum(jnp.where(condition, 1.0, 0.0)).astype(jnp.int32)


def plan_body(frame_count, here, info, sc, starts, ends):
    dur, seg = info[0], info[1]
    n, count = dur.shape
    rows = lax.broadcasted_iota(jnp.int32, (count, count), 0)
    cols = lax.broadcasted_iota(jnp.int32, (count, count), 1)
    upper = jnp.where(rows <= cols, 1.0, 0.0).astype(jnp.bfloat16)
    running = jnp.dot(
        dur.astype(jnp.float32).astype(jnp.bfloat16), upper, preferred_element_type=jnp.float32
    ).astype(jnp.int32)
    sums = jnp.sum(dur.astype(jnp.float32), axis=1, keepdims=True).astype(jnp.int32)
    starts[...] = jnp.zeros_like(starts)
    ends[...] = jnp.zeros_like(ends)
    before = jnp.zeros((1, 1), jnp.int32)
    for r in range(n):
        ends[r : r + 1, :] = running[r : r + 1, :] + before
        before = before + sums[r : r + 1, :]
    done = ends[pl.ds(0, n), :]
    starts[pl.ds(0, n), :] = done - dur
    half = KERNEL // 2
    frame0 = here[0] * frame_count
    first = counted(done <= jnp.maximum(frame0 - half, 0))
    last = counted(done <= jnp.minimum(frame0 + frame_count + half, n * frame_count) - 1)
    base = lax.div(first, ALIGN) * ALIGN
    windows = lax.div(last - base + WIN, WIN)
    sc[0] = jnp.minimum(base, n * count - windows * WIN)
    sc[1] = windows
    sc[2] = frame0
    sc[3] = last
    for v in range(SEGS + 1):
        sc[4 + v] = counted(seg < v)


def load_body(source, target, sems):
    rows = source.shape[0] // LOADS
    copies = []
    for i in range(LOADS):
        part = pl.ds(i * rows, rows)
        copies.append(pltpu.make_async_copy(source.at[part], target.at[part], sems.at[i]))
    for copy in copies:
        copy.start()
    for copy in copies:
        copy.wait()


def load(array):
    return pl.pallas_call(
        load_body,
        out_shape=pltpu.VMEM(array.shape, array.dtype),
        in_specs=[pl.BlockSpec(memory_space=pltpu.HBM)],
        out_specs=pl.BlockSpec(memory_space=pltpu.VMEM),
        scratch_shapes=[pltpu.SemaphoreType.DMA((LOADS,))],
        cost_estimate=pl.CostEstimate(
            flops=0, bytes_accessed=2 * array.size * array.dtype.itemsize, transcendentals=0
        ),
        compiler_params=pltpu.CompilerParams(vmem_limit_bytes=PROJECT_VMEM),
    )(pltpu.with_memory_space_constraint(array, pltpu.HBM))


def project_body(step, dy, outer, here, x0, x1, gain, w, *rest):
    ks, vs, xa, token, hs, sem = rest[-6:]
    rows, width = x0.shape
    slot = lax.rem(lax.div(here[0], 4) + outer - step, outer) * 2 + (lax.rem(lax.div(here[0], 2), 2) ^ dy)
    core = lax.rem(here[0], 2)
    copies = []
    for i, ref in enumerate((x0, x1)):
        start = pl.multiple_of(slot * 2 * rows + (core ^ i) * rows, rows)
        copies.append(pltpu.make_async_copy(ref, xa.at[pl.ds(start, rows)], sem.at[i]))
    for copy in copies:
        copy.start()
    for copy in copies:
        copy.wait()
    pair = pl.ds(pl.multiple_of(slot * 2 * rows, 2 * rows), 2 * rows)
    token[...] = jnp.zeros_like(token)
    hs[...] = rows_normalized(xa[pair, :].astype(jnp.float32), gain[...]).astype(jnp.bfloat16)
    cols = 256
    for c in range(width, 2 * width, cols):
        k = jnp.dot(hs[...], w[:, c : c + cols], preferred_element_type=jnp.float32)
        ks[slot, :, c - width : c - width + cols] = k.astype(jnp.bfloat16)
    for c in range(2 * width, 3 * width, cols):
        v = jnp.dot(hs[...], w[:, c : c + cols], preferred_element_type=jnp.float32)
        vs[slot, c - 2 * width : c - 2 * width + cols, :] = v.astype(jnp.bfloat16).T


def project(step, dy, outer, here, blocks, gain, w_qkv, previous, token, units):
    rows, width = blocks[0].shape
    pair = 2 * rows
    pairs = units // pair
    vmem = pl.BlockSpec(memory_space=pltpu.VMEM)
    any_spec = pl.BlockSpec(memory_space=pl.ANY)
    operands = [here, *blocks, gain, w_qkv]
    in_specs = [pl.BlockSpec(memory_space=pltpu.SMEM), any_spec, any_spec, vmem, vmem]
    if token is not None:
        in_specs += [any_spec]
        operands += [token]
    aliases = {}
    if previous is not None:
        aliases = {len(operands) + i: i for i in range(3)}
        in_specs += [any_spec] * 3
        operands += list(previous)
    return pl.pallas_call(
        functools.partial(project_body, step, dy, outer),
        out_shape=(
            pltpu.VMEM((pairs, pair, width), jnp.bfloat16),
            pltpu.VMEM((pairs, width, pair), jnp.bfloat16),
            pltpu.VMEM((units, width), jnp.bfloat16),
            jax.ShapeDtypeStruct((8, 128), jnp.float32),
        ),
        in_specs=in_specs,
        out_specs=(vmem,) * 4,
        scratch_shapes=[pltpu.VMEM((pair, width), jnp.bfloat16), pltpu.SemaphoreType.DMA((2,))],
        input_output_aliases=aliases,
        cost_estimate=pl.CostEstimate(
            flops=2 * pair * width * 2 * width,
            bytes_accessed=2 * (width * 2 * width + 4 * pair * width),
            transcendentals=0,
        ),
        compiler_params=pltpu.CompilerParams(vmem_limit_bytes=PROJECT_VMEM),
    )(*operands)


def frames_body(
    sc, starts, ends, gain, conv_b, conv_gain, xa, keys, values, w_qkv, w_out, w_proj, conv_w,
    out, wo, wp, cw, xw, qs, bias, acc, acc_rest, tops, totals, turned, red,
    expanded, sems,
):
    width = w_out.shape[0]
    channels = w_proj.shape[1]
    head = width // HEADS
    deep = GROUP * head
    frames = out.shape[0]
    tile = keys.shape[1]
    half = KERNEL // 2
    scale = math.log2(math.e) / math.sqrt(head)

    load_o = pltpu.make_async_copy(w_out, wo, sems.at[1])
    load_p = pltpu.make_async_copy(w_proj, wp, sems.at[2])
    load_c = pltpu.make_async_copy(conv_w, cw, sems.at[3])
    load_o.start()
    load_p.start()
    load_c.start()

    base, windows, frame0 = sc[0], sc[1], sc[2]

    def seg_start(v):
        return sc[4 + v]

    def window(w, carry):
        r0 = pl.multiple_of(base + w * WIN, ALIGN)
        load_x = pltpu.make_async_copy(xa.at[pl.ds(r0, WIN)], xw, sems.at[4])
        load_x.start()
        lo, hi = jnp.int32(0), jnp.int32(0)
        for v in range(SEGS):
            lo = jnp.where(r0 >= seg_start(v), seg_start(v), lo)
            hi = jnp.where(r0 + WIN - 1 >= seg_start(v), seg_start(v + 1), hi)
        t0 = lax.div(lo, tile)
        t1 = lax.div(hi + tile - 1, tile)

        load_x.wait()
        h = rows_normalized(xw[...].astype(jnp.float32), gain[...]).astype(jnp.bfloat16)
        q = jnp.dot(h, w_qkv[:, :width], preferred_element_type=jnp.float32).astype(jnp.bfloat16)
        owner = lax.broadcasted_iota(jnp.int32, (WIN, deep), 1) // head
        zero = jnp.zeros((WIN, deep), jnp.bfloat16)
        for g in range(HEADS // GROUP):
            part = q[:, g * deep : (g + 1) * deep]
            for j in range(GROUP):
                alone = jnp.where(owner == j, part, zero)
                qs[g, j * MAIN : (j + 1) * MAIN, :] = alone[:MAIN]
                start = GROUP * MAIN + j * REST
                qs[g, start : start + REST, :] = alone[MAIN:]
        acc[...] = jnp.zeros_like(acc)
        acc_rest[...] = jnp.zeros_like(acc_rest)
        tops[...] = jnp.full_like(tops, LOW)
        totals[...] = jnp.zeros_like(totals)

        lane = lax.broadcasted_iota(jnp.int32, (1, 2 * MAIN), 1)
        row = r0 + jnp.where(lane < MAIN, lane, MAIN + (lane - MAIN) % REST)
        row_lo = jnp.zeros_like(row)
        row_hi = jnp.zeros_like(row)
        for v in range(SEGS):
            row_lo = jnp.where(row >= seg_start(v), seg_start(v), row_lo)
            row_hi = jnp.where(row >= seg_start(v), seg_start(v + 1), row_hi)

        def key_step(t, c):
            key = t * tile + lax.broadcasted_iota(jnp.int32, (tile, 2 * MAIN), 0)
            bias[...] = jnp.where((key >= row_lo) & (key < row_hi), 0.0, MASKED)
            main = bias[:, :MAIN]
            mask = jnp.concatenate([main] * GROUP + [bias[:, MAIN:]], axis=1)
            for g in range(HEADS // GROUP):
                dims = slice(g * deep, (g + 1) * deep)
                s = lax.dot_general(
                    keys[t, :, dims], qs[g], (((1,), (1,)), ((), ())),
                    preferred_element_type=jnp.float32,
                )
                s = s * scale + mask
                top = tops[g]
                new_top = jnp.maximum(top, jnp.max(s, axis=0, keepdims=True))
                expo = jnp.exp2(s - new_top)
                alpha = jnp.exp2(top - new_top)
                tops[g] = new_top
                totals[g] = totals[g] * alpha + jnp.sum(expo, axis=0, keepdims=True)
                expo = expo.astype(jnp.bfloat16)
                for j in range(GROUP):
                    lanes = slice(j * MAIN, (j + 1) * MAIN)
                    start = g * deep + j * head
                    acc[g, j] = acc[g, j] * alpha[:, lanes] + jnp.dot(
                        values[t, start : start + head, :], expo[:, lanes],
                        preferred_element_type=jnp.float32,
                    )
                acc_rest[g] = acc_rest[g] * alpha[:, GROUP * MAIN :] + jnp.dot(
                    values[t, dims, :], expo[:, GROUP * MAIN :],
                    preferred_element_type=jnp.float32,
                )
            return c

        lax.fori_loop(t0, t1, key_step, 0)

        for g in range(HEADS // GROUP):
            total = totals[g]
            total = jnp.where(total == 0.0, 1.0, total)
            for j in range(GROUP):
                start = g * deep + j * head
                lanes = slice(j * MAIN, (j + 1) * MAIN)
                turned[start : start + head, :MAIN] = acc[g, j] / total[:, lanes]
            rest = acc_rest[g] / total[:, GROUP * MAIN :]
            for j in range(GROUP):
                start = g * deep + j * head
                turned[start : start + head, MAIN:WIN] = rest[
                    j * head : (j + 1) * head, j * REST : (j + 1) * REST
                ]
        attended = turned[...].T[:WIN].astype(jnp.bfloat16)

        @pl.when(w == 0)
        def _():
            load_o.wait()
            load_p.wait()

        mixed = jnp.dot(attended, wo[...], preferred_element_type=jnp.float32) + xw[...].astype(
            jnp.float32
        )
        reduced = jnp.dot(
            mixed.astype(jnp.bfloat16), wp[...], preferred_element_type=jnp.float32
        ).astype(jnp.bfloat16)
        red[pl.ds(0, WIN), :] = reduced
        red[pl.ds(WIN, LANES - WIN), :] = jnp.zeros((LANES - WIN, channels), jnp.bfloat16)
        shape = (frames + 2 * HALO, LANES)
        frame = frame0 - HALO + lax.broadcasted_iota(jnp.int32, shape, 0)
        lanes = starts.shape[1]
        row0 = lax.div(r0, lanes)
        shift = 3 * lanes - lax.rem(r0, lanes)

        def cut(ref):
            line = jnp.concatenate([ref[pl.ds(row0 + i, 1), :] for i in range(3)], axis=1)
            line = pltpu.roll(jnp.broadcast_to(line, (8, 3 * lanes)), shift, 1)[:1, :LANES]
            return jnp.where(lax.broadcasted_iota(jnp.int32, (1, LANES), 1) < WIN, line, 0)

        pick = jnp.where((frame >= cut(starts)) & (frame < cut(ends)), 1.0, 0.0).astype(jnp.bfloat16)
        rows = jnp.dot(pick, red[...], preferred_element_type=jnp.float32)

        @pl.when(w == 0)
        def _():
            expanded[...] = rows

        @pl.when(w > 0)
        def _():
            expanded[...] += rows

        return carry

    lax.fori_loop(0, windows, window, 0)

    load_c.wait()
    block = 256
    for b in range(frames // block):
        conv = jnp.zeros((block, channels), jnp.float32) + conv_b[...]
        for tap in range(KERNEL):
            part = expanded[pl.ds(b * block + HALO - half + tap, block), :].astype(jnp.bfloat16)
            conv = conv + jnp.dot(part, cw[tap], preferred_element_type=jnp.float32)
        result = expanded[pl.ds(b * block + HALO, block), :] + rows_normalized(
            jnp.maximum(conv, 0.0), conv_gain[...]
        )
        out[pl.ds(b * block, block), :] = result.astype(jnp.bfloat16)


def frames_call(sc, starts, ends, gain, conv_b, conv_gain, xa, ks, vs, w_qkv, w_out, w_proj, conv_w, frames):
    units, width = xa.shape
    channels = w_proj.shape[1]
    head = width // HEADS
    hbm = pl.BlockSpec(memory_space=pltpu.HBM)
    vmem = pl.BlockSpec(memory_space=pltpu.VMEM)
    groups = HEADS // GROUP
    return pl.pallas_call(
        frames_body,
        out_shape=jax.ShapeDtypeStruct((frames, channels), jnp.bfloat16),
        in_specs=[pl.BlockSpec(memory_space=pltpu.SMEM)] + [vmem] * 9 + [hbm] * 3,
        out_specs=vmem,
        scratch_shapes=[
            pltpu.VMEM((width, width), jnp.bfloat16),
            pltpu.VMEM((width, channels), jnp.bfloat16),
            pltpu.VMEM((KERNEL, channels, channels), jnp.bfloat16),
            pltpu.VMEM((WIN, width), jnp.bfloat16),
            pltpu.VMEM((groups, STACK, GROUP * head), jnp.bfloat16),
            pltpu.VMEM((ks.shape[1], 2 * MAIN), jnp.float32),
            pltpu.VMEM((groups, GROUP, head, MAIN), jnp.float32),
            pltpu.VMEM((groups, GROUP * head, GROUP * REST), jnp.float32),
            pltpu.VMEM((groups, 1, STACK), jnp.float32),
            pltpu.VMEM((groups, 1, STACK), jnp.float32),
            pltpu.VMEM((width, 2 * MAIN), jnp.float32),
            pltpu.VMEM((LANES, channels), jnp.bfloat16),
            pltpu.VMEM((frames + 2 * HALO, channels), jnp.float32),
            pltpu.SemaphoreType.DMA((5,)),
        ],
        compiler_params=pltpu.CompilerParams(vmem_limit_bytes=FRAMES_VMEM),
    )(sc, starts, ends, gain, conv_b, conv_gain, xa, ks, vs, w_qkv, w_out, w_proj, conv_w)


def local(units, durations, seg_ids, ln_gain, w_qkv, w_out, w_proj, conv_w, conv_b, conv_gain):
    n = lax.axis_size("seq")
    outer = n // 4
    here = lax.axis_index("seq")
    count = units.shape[0]
    total = n * count
    frame_count = DUR_MEAN * count

    def place(z, y, c):
        return (z * 2 + y) * 2 + c

    def pairs(step, dy, dc):
        return [
            (place(z, y, c), place((z + step) % outer, y ^ dy, c ^ dc))
            for z in range(outer)
            for y in range(2)
            for c in range(2)
        ]

    def send(value, step, dy=0, dc=0):
        return lax.ppermute(value, "seq", pairs(step, dy, dc))

    gain = ln_gain[None, :]
    w_out, w_proj, conv_w = [
        pltpu.with_memory_space_constraint(w, pltpu.HBM) for w in (w_out, w_proj, conv_w)
    ]
    where = here.reshape(1)
    shape = jax.ShapeDtypeStruct((2, n, count), jnp.int32)

    def join(*arrays):
        return small_call(join_body, shape, where, *arrays)

    w_qkv = load(w_qkv)

    info = small_call(place_body, shape, where, durations[None, :], seg_ids[None, :])

    hops = [(0, 0, 1), (0, 1, 0)]
    if outer & (outer - 1) == 0:
        hops += [(1 << i, 0, 0) for i in range(outer.bit_length() - 1)]
    else:
        hops += [None]

    def spread(info, token):
        token, info = lax.optimization_barrier((token, info))
        hop = hops.pop(0)
        if hop is None:
            return token, join(info, *[send(info, s) for s in range(1, outer)])
        return token, join(info, send(info, *hop))

    state = token = None
    block = units
    waiting = None
    for step in range(outer):
        following = send(block, 1) if step < outer - 1 else None
        across = send(block, 0, 1, 0)
        beside = send(block, 0, 0, 1)
        if waiting is not None:
            *state, token = project(*waiting, gain, w_qkv, state, token, total)
            if hops:
                token, info = spread(info, token)
        *state, token = project(step, 0, outer, where, (block, beside), gain, w_qkv, state, token, total)
        token, across = lax.optimization_barrier((token, across))
        diagonal = send(across, 0, 0, 1)
        if step == 0:
            token, info = spread(info, token)
        if following is not None:
            token, following, info = lax.optimization_barrier((token, following, info))
        waiting = (step, 1, outer, where, (across, diagonal))
        block = following
    while hops:
        token, info = spread(info, token)
    *state, token = project(*waiting, gain, w_qkv, state, token, total)

    edge = jax.ShapeDtypeStruct((n + 8, count), jnp.int32)
    sc, starts, ends = pl.pallas_call(
        functools.partial(plan_body, frame_count),
        out_shape=(jax.ShapeDtypeStruct((SEGS + 5,), jnp.int32), edge, edge),
        in_specs=[pl.BlockSpec(memory_space=pltpu.SMEM), pl.BlockSpec(memory_space=pltpu.VMEM)],
        out_specs=(
            pl.BlockSpec(memory_space=pltpu.SMEM),
            pl.BlockSpec(memory_space=pltpu.VMEM),
            pl.BlockSpec(memory_space=pltpu.VMEM),
        ),
        compiler_params=pltpu.CompilerParams(vmem_limit_bytes=SMALL_VMEM),
    )(where, info)
    ks, vs, xa = state
    return frames_call(
        sc, starts, ends, gain, conv_b[None, :], conv_gain[None, :], xa, ks, vs, w_qkv, w_out,
        w_proj, conv_w, frame_count,
    )


def solution(mesh):
    split = P(("grp", "seq"))
    in_specs = (P(("grp", "seq"), None), split, split) + (P(),) * 7
    return jax.shard_map(
        local, mesh=mesh, in_specs=in_specs, out_specs=P(("grp", "seq"), None), check_vma=False
    )
```

```python
import functools
import math

import jax
import jax.numpy as jnp
from jax import lax
from jax.experimental import pallas as pl
from jax.experimental.pallas import tpu as pltpu
from jax.sharding import PartitionSpec as P


HEADS = 16
KERNEL = 5
SEGS = 8
DUR_MEAN = 6
EPS = 1e-05

MAIN = 128
REST = 32
WIN = MAIN + REST
GROUP = 4
STACK = GROUP * WIN
ALIGN = 8
LANES = 256
HALO = 8
LOW = -1e30
MASKED = -2e30
LOADS = 8
SMALL_VMEM = 4 << 20
EXTRA = 8
PROJECT_VMEM = 6 << 20
FRAMES_VMEM = 24 << 20


def rows_normalized(values, gain):
    mean = jnp.mean(values, axis=-1, keepdims=True)
    centred = values - mean
    variance = jnp.mean(centred * centred, axis=-1, keepdims=True)
    return centred * lax.rsqrt(variance + EPS) * gain


def pack_body(here, units, dur, seg, out, ids, sems):
    rows, width = units.shape
    count = dur.shape[1]
    copies = [
        pltpu.make_async_copy(dur, ids.at[:, pl.ds(0, count)], sems.at[0]),
        pltpu.make_async_copy(seg, ids.at[:, pl.ds(count, count)], sems.at[1]),
        pltpu.make_async_copy(units, out.at[pl.ds(0, rows)], sems.at[2]),
    ]
    for copy in copies:
        copy.start()
    out[pl.ds(rows, EXTRA), :] = jnp.zeros((EXTRA, width), jnp.bfloat16)
    copies[0].wait()
    copies[1].wait()
    line = ids[...].astype(jnp.float32).astype(jnp.bfloat16)
    out[pl.ds(rows, EXTRA), : 2 * count] = jnp.broadcast_to(line, (EXTRA, 2 * count))
    copies[2].wait()


def pack(here, units, dur, seg):
    rows, width = units.shape
    hbm = pl.BlockSpec(memory_space=pltpu.HBM)
    arrays = [pltpu.with_memory_space_constraint(array, pltpu.HBM) for array in (units, dur, seg)]
    return pl.pallas_call(
        pack_body,
        out_shape=jax.ShapeDtypeStruct((rows + EXTRA, width), units.dtype),
        in_specs=[pl.BlockSpec(memory_space=pltpu.SMEM), hbm, hbm, hbm],
        out_specs=pl.BlockSpec(memory_space=pltpu.VMEM),
        scratch_shapes=[
            pltpu.VMEM((1, 2 * dur.shape[1]), jnp.int32), pltpu.SemaphoreType.DMA((3,))
        ],
        compiler_params=pltpu.CompilerParams(vmem_limit_bytes=SMALL_VMEM),
    )(here, *arrays)


def counted(condition):
    return jnp.sum(jnp.where(condition, 1.0, 0.0)).astype(jnp.int32)


def plan(frame_count, here, meta, sc, lines, starts, ends):
    n, _, double = meta.shape
    count = double // 2
    for i in range(n):
        lines[i : i + 1, :] = meta[i].astype(jnp.float32)[:1]
    dur, seg = lines[:, :count], lines[:, count:]
    rows = lax.broadcasted_iota(jnp.int32, (count, count), 0)
    cols = lax.broadcasted_iota(jnp.int32, (count, count), 1)
    upper = jnp.where(rows <= cols, 1.0, 0.0).astype(jnp.bfloat16)
    running = jnp.dot(dur.astype(jnp.bfloat16), upper, preferred_element_type=jnp.float32)
    sums = jnp.sum(dur, axis=1, keepdims=True)
    starts[...] = jnp.zeros_like(starts)
    ends[...] = jnp.zeros_like(ends)
    before = jnp.zeros((1, 1), jnp.float32)
    for r in range(n):
        ends[r : r + 1, :] = (running[r : r + 1, :] + before).astype(jnp.int32)
        before = before + sums[r : r + 1, :]
    done = ends[pl.ds(0, n), :]
    starts[pl.ds(0, n), :] = done - dur.astype(jnp.int32)
    half = KERNEL // 2
    frame0 = here * frame_count
    first = counted(done <= jnp.maximum(frame0 - half, 0))
    last = counted(done <= jnp.minimum(frame0 + frame_count + half, n * frame_count) - 1)
    base = lax.div(first, ALIGN) * ALIGN
    windows = lax.div(last - base + WIN, WIN)
    sc[0] = jnp.minimum(base, n * count - windows * WIN)
    sc[1] = windows
    sc[2] = frame0
    for v in range(SEGS + 1):
        sc[4 + v] = counted(seg < v)


def load_body(here, source, target, token, sems):
    token[...] = jnp.zeros_like(token)
    rows = source.shape[0] // LOADS
    copies = []
    for i in range(LOADS):
        part = pl.ds(i * rows, rows)
        copies.append(pltpu.make_async_copy(source.at[part], target.at[part], sems.at[i]))
    for copy in copies:
        copy.start()
    for copy in copies:
        copy.wait()


def load(here, array):
    return pl.pallas_call(
        load_body,
        out_shape=(
            pltpu.VMEM(array.shape, array.dtype), jax.ShapeDtypeStruct((8, 128), jnp.float32)
        ),
        in_specs=[pl.BlockSpec(memory_space=pltpu.SMEM), pl.BlockSpec(memory_space=pltpu.HBM)],
        out_specs=(pl.BlockSpec(memory_space=pltpu.VMEM),) * 2,
        scratch_shapes=[pltpu.SemaphoreType.DMA((LOADS,))],
        cost_estimate=pl.CostEstimate(
            flops=0, bytes_accessed=2 * array.size * array.dtype.itemsize, transcendentals=0
        ),
        compiler_params=pltpu.CompilerParams(vmem_limit_bytes=PROJECT_VMEM),
    )(here, pltpu.with_memory_space_constraint(array, pltpu.HBM))


def project_body(step, dy, outer, here, x0, x1, gain, w, *rest):
    ks, vs, xa, meta, token, hs, sem = rest[-7:]
    rows, width = x0.shape
    rows = rows - EXTRA
    slot = lax.rem(lax.div(here[0], 4) + outer - step, outer) * 2 + (lax.rem(lax.div(here[0], 2), 2) ^ dy)
    core = lax.rem(here[0], 2)
    copies = []
    for i, ref in enumerate((x0, x1)):
        start = pl.multiple_of(slot * 2 * rows + (core ^ i) * rows, rows)
        copies.append(
            pltpu.make_async_copy(ref.at[pl.ds(0, rows)], xa.at[pl.ds(start, rows)], sem.at[i])
        )
        ids = ref.at[pl.ds(rows, EXTRA), pl.ds(0, meta.shape[2])]
        copies.append(pltpu.make_async_copy(ids, meta.at[slot * 2 + (core ^ i)], sem.at[2 + i]))
    for copy in copies:
        copy.start()
    for copy in copies:
        copy.wait()
    pair = pl.ds(pl.multiple_of(slot * 2 * rows, 2 * rows), 2 * rows)
    token[...] = jnp.zeros_like(token)
    hs[...] = rows_normalized(xa[pair, :].astype(jnp.float32), gain[...]).astype(jnp.bfloat16)
    cols = 256
    for c in range(width, 2 * width, cols):
        k = jnp.dot(hs[...], w[:, c : c + cols], preferred_element_type=jnp.float32)
        ks[slot, :, c - width : c - width + cols] = k.astype(jnp.bfloat16)
    for c in range(2 * width, 3 * width, cols):
        v = jnp.dot(hs[...], w[:, c : c + cols], preferred_element_type=jnp.float32)
        vs[slot, c - 2 * width : c - 2 * width + cols, :] = v.astype(jnp.bfloat16).T


def project(step, dy, outer, here, blocks, gain, w_qkv, previous, after, units):
    rows, width = blocks[0].shape
    rows = rows - EXTRA
    pair = 2 * rows
    pairs = units // pair
    vmem = pl.BlockSpec(memory_space=pltpu.VMEM)
    any_spec = pl.BlockSpec(memory_space=pl.ANY)
    operands = [here, *blocks, gain, w_qkv]
    in_specs = [pl.BlockSpec(memory_space=pltpu.SMEM), any_spec, any_spec, vmem, vmem]
    in_specs += [any_spec] * len(after)
    operands += list(after)
    aliases = {}
    if previous is not None:
        aliases = {len(operands) + i: i for i in range(4)}
        in_specs += [any_spec] * 4
        operands += list(previous)
    return pl.pallas_call(
        functools.partial(project_body, step, dy, outer),
        out_shape=(
            pltpu.VMEM((pairs, pair, width), jnp.bfloat16),
            pltpu.VMEM((pairs, width, pair), jnp.bfloat16),
            pltpu.VMEM((units, width), jnp.bfloat16),
            pltpu.VMEM((units // rows, EXTRA, 2 * rows), jnp.bfloat16),
            jax.ShapeDtypeStruct((8, 128), jnp.float32),
        ),
        in_specs=in_specs,
        out_specs=(vmem,) * 5,
        scratch_shapes=[pltpu.VMEM((pair, width), jnp.bfloat16), pltpu.SemaphoreType.DMA((4,))],
        input_output_aliases=aliases,
        cost_estimate=pl.CostEstimate(
            flops=2 * pair * width * 2 * width,
            bytes_accessed=2 * (width * 2 * width + 4 * pair * width),
            transcendentals=0,
        ),
        compiler_params=pltpu.CompilerParams(vmem_limit_bytes=PROJECT_VMEM),
    )(*operands)


def frames_body(
    here, meta, gain, conv_b, conv_gain, xa, keys, values, w_qkv, w_out, w_proj, conv_w,
    out, wo, wp, cw, xw, qs, begun, bias, acc, acc_rest, tops, totals, turned, red,
    expanded, sc, lines, starts, ends, sems,
):
    width = w_out.shape[0]
    channels = w_proj.shape[1]
    head = width // HEADS
    deep = GROUP * head
    frames = out.shape[0]
    tile = keys.shape[1]
    half = KERNEL // 2
    scale = math.log2(math.e) / math.sqrt(head)

    load_o = pltpu.make_async_copy(w_out, wo, sems.at[1])
    load_p = pltpu.make_async_copy(w_proj, wp, sems.at[2])
    load_c = pltpu.make_async_copy(conv_w, cw, sems.at[3])
    load_o.start()
    load_p.start()
    load_c.start()

    plan(frames, here[0], meta, sc, lines, starts, ends)
    base, windows, frame0 = sc[0], sc[1], sc[2]

    def seg_start(v):
        return sc[4 + v]

    def window(w, carry):
        r0 = pl.multiple_of(base + w * WIN, ALIGN)
        load_x = pltpu.make_async_copy(xa.at[pl.ds(r0, WIN)], xw, sems.at[4])
        load_x.start()
        lo, hi = jnp.int32(0), jnp.int32(0)
        for v in range(SEGS):
            lo = jnp.where(r0 >= seg_start(v), seg_start(v), lo)
            hi = jnp.where(r0 + WIN - 1 >= seg_start(v), seg_start(v + 1), hi)
        t0 = lax.div(lo, tile)
        t1 = lax.div(hi + tile - 1, tile)

        load_x.wait()
        h = rows_normalized(xw[...].astype(jnp.float32), gain[...]).astype(jnp.bfloat16)
        q = jnp.dot(h, w_qkv[:, :width], preferred_element_type=jnp.float32).astype(jnp.bfloat16)
        owner = lax.broadcasted_iota(jnp.int32, (WIN, deep), 1) // head
        zero = jnp.zeros((WIN, deep), jnp.bfloat16)
        for g in range(HEADS // GROUP):
            part = q[:, g * deep : (g + 1) * deep]
            for j in range(GROUP):
                alone = jnp.where(owner == j, part, zero)
                qs[g, j * MAIN : (j + 1) * MAIN, :] = alone[:MAIN]
                start = GROUP * MAIN + j * REST
                qs[g, start : start + REST, :] = alone[MAIN:]
        acc[...] = jnp.zeros_like(acc)
        acc_rest[...] = jnp.zeros_like(acc_rest)
        tops[...] = jnp.full_like(tops, LOW)
        totals[...] = jnp.zeros_like(totals)

        lane = lax.broadcasted_iota(jnp.int32, (1, 2 * MAIN), 1)
        row = r0 + jnp.where(lane < MAIN, lane, MAIN + (lane - MAIN) % REST)
        row_lo = jnp.zeros_like(row)
        row_hi = jnp.zeros_like(row)
        for v in range(SEGS):
            row_lo = jnp.where(row >= seg_start(v), seg_start(v), row_lo)
            row_hi = jnp.where(row >= seg_start(v), seg_start(v + 1), row_hi)

        def scores(t, g):
            dims = slice(g * deep, (g + 1) * deep)
            return lax.dot_general(
                keys[t, :, dims], qs[g], (((1,), (1,)), ((), ())),
                preferred_element_type=jnp.float32,
            )

        begun[...] = scores(t0, 0)

        def key_step(t, c):
            key = t * tile + lax.broadcasted_iota(jnp.int32, (tile, 2 * MAIN), 0)
            bias[...] = jnp.where((key >= row_lo) & (key < row_hi), 0.0, MASKED)
            main = bias[:, :MAIN]
            mask = jnp.concatenate([main] * GROUP + [bias[:, MAIN:]], axis=1)
            groups = HEADS // GROUP

            ahead = begun[...]
            for g in range(groups):
                dims = slice(g * deep, (g + 1) * deep)
                s = ahead * scale + mask
                if g + 1 < groups:
                    ahead = scores(t, g + 1)
                else:
                    begun[...] = scores(jnp.minimum(t + 1, t1 - 1), 0)
                top = tops[g]
                new_top = jnp.maximum(top, jnp.max(s, axis=0, keepdims=True))
                expo = jnp.exp2(s - new_top)
                alpha = jnp.exp2(top - new_top)
                tops[g] = new_top
                totals[g] = totals[g] * alpha + jnp.sum(expo, axis=0, keepdims=True)
                expo = expo.astype(jnp.bfloat16)
                for j in range(GROUP):
                    lanes = slice(j * MAIN, (j + 1) * MAIN)
                    start = g * deep + j * head
                    acc[g, j] = acc[g, j] * alpha[:, lanes] + jnp.dot(
                        values[t, start : start + head, :], expo[:, lanes],
                        preferred_element_type=jnp.float32,
                    )
                acc_rest[g] = acc_rest[g] * alpha[:, GROUP * MAIN :] + jnp.dot(
                    values[t, dims, :], expo[:, GROUP * MAIN :],
                    preferred_element_type=jnp.float32,
                )
            return c

        lax.fori_loop(t0, t1, key_step, 0)

        for g in range(HEADS // GROUP):
            total = totals[g]
            total = jnp.where(total == 0.0, 1.0, total)
            for j in range(GROUP):
                start = g * deep + j * head
                lanes = slice(j * MAIN, (j + 1) * MAIN)
                turned[start : start + head, :MAIN] = acc[g, j] / total[:, lanes]
            rest = acc_rest[g] / total[:, GROUP * MAIN :]
            for j in range(GROUP):
                start = g * deep + j * head
                turned[start : start + head, MAIN:WIN] = rest[
                    j * head : (j + 1) * head, j * REST : (j + 1) * REST
                ]
        attended = turned[...].T[:WIN].astype(jnp.bfloat16)

        @pl.when(w == 0)
        def _():
            load_o.wait()
            load_p.wait()

        mixed = jnp.dot(attended, wo[...], preferred_element_type=jnp.float32) + xw[...].astype(
            jnp.float32
        )
        reduced = jnp.dot(
            mixed.astype(jnp.bfloat16), wp[...], preferred_element_type=jnp.float32
        ).astype(jnp.bfloat16)
        red[pl.ds(0, WIN), :] = reduced
        red[pl.ds(WIN, LANES - WIN), :] = jnp.zeros((LANES - WIN, channels), jnp.bfloat16)
        shape = (frames + 2 * HALO, LANES)
        frame = frame0 - HALO + lax.broadcasted_iota(jnp.int32, shape, 0)
        lanes = starts.shape[1]
        row0 = lax.div(r0, lanes)
        shift = 3 * lanes - lax.rem(r0, lanes)

        def cut(ref):
            line = jnp.concatenate([ref[pl.ds(row0 + i, 1), :] for i in range(3)], axis=1)
            line = pltpu.roll(jnp.broadcast_to(line, (8, 3 * lanes)), shift, 1)[:1, :LANES]
            return jnp.where(lax.broadcasted_iota(jnp.int32, (1, LANES), 1) < WIN, line, 0)

        pick = jnp.where((frame >= cut(starts)) & (frame < cut(ends)), 1.0, 0.0).astype(jnp.bfloat16)
        rows = jnp.dot(pick, red[...], preferred_element_type=jnp.float32)

        @pl.when(w == 0)
        def _():
            expanded[...] = rows

        @pl.when(w > 0)
        def _():
            expanded[...] += rows

        return carry

    lax.fori_loop(0, windows, window, 0)

    load_c.wait()
    block = 256
    for b in range(frames // block):
        conv = jnp.zeros((block, channels), jnp.float32) + conv_b[...]
        for tap in range(KERNEL):
            part = expanded[pl.ds(b * block + HALO - half + tap, block), :].astype(jnp.bfloat16)
            conv = conv + jnp.dot(part, cw[tap], preferred_element_type=jnp.float32)
        result = expanded[pl.ds(b * block + HALO, block), :] + rows_normalized(
            jnp.maximum(conv, 0.0), conv_gain[...]
        )
        out[pl.ds(b * block, block), :] = result.astype(jnp.bfloat16)


def frames_call(here, meta, gain, conv_b, conv_gain, xa, ks, vs, w_qkv, w_out, w_proj, conv_w, frames):
    _, width = xa.shape
    channels = w_proj.shape[1]
    head = width // HEADS
    hbm = pl.BlockSpec(memory_space=pltpu.HBM)
    vmem = pl.BlockSpec(memory_space=pltpu.VMEM)
    groups = HEADS // GROUP
    return pl.pallas_call(
        frames_body,
        out_shape=jax.ShapeDtypeStruct((frames, channels), jnp.bfloat16),
        in_specs=[pl.BlockSpec(memory_space=pltpu.SMEM)] + [vmem] * 8 + [hbm] * 3,
        out_specs=vmem,
        scratch_shapes=[
            pltpu.VMEM((width, width), jnp.bfloat16),
            pltpu.VMEM((width, channels), jnp.bfloat16),
            pltpu.VMEM((KERNEL, channels, channels), jnp.bfloat16),
            pltpu.VMEM((WIN, width), jnp.bfloat16),
            pltpu.VMEM((groups, STACK, GROUP * head), jnp.bfloat16),
            pltpu.VMEM((ks.shape[1], STACK), jnp.float32),
            pltpu.VMEM((ks.shape[1], 2 * MAIN), jnp.float32),
            pltpu.VMEM((groups, GROUP, head, MAIN), jnp.float32),
            pltpu.VMEM((groups, GROUP * head, GROUP * REST), jnp.float32),
            pltpu.VMEM((groups, 1, STACK), jnp.float32),
            pltpu.VMEM((groups, 1, STACK), jnp.float32),
            pltpu.VMEM((width, 2 * MAIN), jnp.float32),
            pltpu.VMEM((LANES, channels), jnp.bfloat16),
            pltpu.VMEM((frames + 2 * HALO, channels), jnp.float32),
            pltpu.SMEM((SEGS + 5,), jnp.int32),
            pltpu.VMEM((meta.shape[0], meta.shape[2]), jnp.float32),
            pltpu.VMEM((meta.shape[0] + 8, meta.shape[2] // 2), jnp.int32),
            pltpu.VMEM((meta.shape[0] + 8, meta.shape[2] // 2), jnp.int32),
            pltpu.SemaphoreType.DMA((5,)),
        ],
        compiler_params=pltpu.CompilerParams(vmem_limit_bytes=FRAMES_VMEM),
    )(here, meta, gain, conv_b, conv_gain, xa, ks, vs, w_qkv, w_out, w_proj, conv_w)


def local(units, durations, seg_ids, ln_gain, w_qkv, w_out, w_proj, conv_w, conv_b, conv_gain):
    n = lax.axis_size("seq")
    outer = n // 4
    here = lax.axis_index("seq")
    count = units.shape[0]
    total = n * count
    frame_count = DUR_MEAN * count

    def place(z, y, c):
        return (z * 2 + y) * 2 + c

    def pairs(step, dy, dc):
        return [
            (place(z, y, c), place((z + step) % outer, y ^ dy, c ^ dc))
            for z in range(outer)
            for y in range(2)
            for c in range(2)
        ]

    def send(value, step, dy=0, dc=0):
        return lax.ppermute(value, "seq", pairs(step, dy, dc))

    gain = ln_gain[None, :]
    w_out, w_proj, conv_w = [
        pltpu.with_memory_space_constraint(w, pltpu.HBM) for w in (w_out, w_proj, conv_w)
    ]
    where = here.reshape(1)

    def kernel(distance, dy, blocks, state, *after):
        *state, token = project(
            distance % outer, dy, outer, where, blocks, gain, w_qkv, state, after, total
        )
        return state, token

    w_qkv, token = load(where, w_qkv)
    state = None
    far_up, far_down = outer // 2, (outer - 1) // 2
    up = down = own = pack(where, units, durations[None, :], seg_ids[None, :])
    arrived = [(0, own)]
    waiting = []
    for step in range(far_up + 1):
        following = []
        if step < far_up:
            up = send(up, 1)
            following.append((step + 1, up))
        if step < far_down:
            down = send(down, outer - 1)
            following.append((-(step + 1), down))
        for pair in waiting:
            state, token = kernel(*pair, state, token)
        if waiting and following:
            held = lax.optimization_barrier((token, *[block for _, block in arrived]))
            token = held[0]
            arrived = [(d, block) for (d, _), block in zip(arrived, held[1:])]
        sides = []
        for d, block in arrived:
            if step == far_up and step > 1:
                across = send(waiting_up, 1)
            else:
                across = send(block, 0, 1, 0)
            sides.append((d, block, across, send(block, 0, 0, 1)))
        for d, block, across, beside in sides:
            state, token = kernel(d, 0, (block, beside), state, token)
        if step == 0:
            ((d, _, across, _),) = sides
            token, across = lax.optimization_barrier((token, across))
            diagonal = send(across, 0, 0, 1)
            state, token = kernel(d, 1, (across, diagonal), state, token)
        halves = [across for _, _, across, _ in sides]
        if following:
            held = lax.optimization_barrier((token, *[block for _, block in following]))
            token = held[0]
            following = [(d, block) for (d, _), block in zip(following, held[1:])]
            up = following[0][1]
            down = following[1][1] if len(following) > 1 else None
        waiting = []
        for (d, _, _, _), across in zip(sides if step > 0 else (), halves):
            token, across = lax.optimization_barrier((token, across))
            waiting.append((d, 1, (across, send(across, 0, 0, 1))))
        waiting_up = sides[0][2]
        arrived = following
    for pair in waiting:
        state, token = kernel(*pair, state, token)

    ks, vs, xa, meta = state
    return frames_call(
        where, meta, gain, conv_b[None, :], conv_gain[None, :], xa, ks, vs, w_qkv, w_out, w_proj,
        conv_w, frame_count,
    )


def solution(mesh):
    split = P(("grp", "seq"))
    in_specs = (P(("grp", "seq"), None), split, split) + (P(),) * 7
    return jax.shard_map(
        local, mesh=mesh, in_specs=in_specs, out_specs=P(("grp", "seq"), None), check_vma=False
    )
```

```python
import functools
import math

import jax
import jax.numpy as jnp
from jax import lax
from jax.experimental import pallas as pl
from jax.experimental.pallas import tpu as pltpu
from jax.sharding import PartitionSpec as P


HEADS = 16
KERNEL = 5
SEGS = 8
DUR_MEAN = 6
EPS = 1e-05

MAIN = 128
REST = 32
WIN = MAIN + REST
GROUP = 4
STACK = GROUP * WIN
ALIGN = 8
LANES = 256
HALO = 8
LOW = -1e30
MASKED = -2e30
LOADS = 8
SMALL_VMEM = 4 << 20
EXTRA = 8
PROJECT_VMEM = 6 << 20
FRAMES_VMEM = 24 << 20


def rows_normalized(values, gain):
    mean = jnp.mean(values, axis=-1, keepdims=True)
    centred = values - mean
    variance = jnp.mean(centred * centred, axis=-1, keepdims=True)
    return centred * lax.rsqrt(variance + EPS) * gain


def pack_body(here, units, dur, seg, out, ids, sems):
    rows, width = units.shape
    count = dur.shape[1]
    copies = [
        pltpu.make_async_copy(dur, ids.at[:, pl.ds(0, count)], sems.at[0]),
        pltpu.make_async_copy(seg, ids.at[:, pl.ds(count, count)], sems.at[1]),
        pltpu.make_async_copy(units, out.at[pl.ds(0, rows)], sems.at[2]),
    ]
    for copy in copies:
        copy.start()
    out[pl.ds(rows, EXTRA), :] = jnp.zeros((EXTRA, width), jnp.bfloat16)
    copies[0].wait()
    copies[1].wait()
    line = ids[...].astype(jnp.float32).astype(jnp.bfloat16)
    out[pl.ds(rows, EXTRA), : 2 * count] = jnp.broadcast_to(line, (EXTRA, 2 * count))
    copies[2].wait()


def pack(here, units, dur, seg):
    rows, width = units.shape
    hbm = pl.BlockSpec(memory_space=pltpu.HBM)
    arrays = [pltpu.with_memory_space_constraint(array, pltpu.HBM) for array in (units, dur, seg)]
    return pl.pallas_call(
        pack_body,
        out_shape=jax.ShapeDtypeStruct((rows + EXTRA, width), units.dtype),
        in_specs=[pl.BlockSpec(memory_space=pltpu.SMEM), hbm, hbm, hbm],
        out_specs=pl.BlockSpec(memory_space=pltpu.VMEM),
        scratch_shapes=[
            pltpu.VMEM((1, 2 * dur.shape[1]), jnp.int32), pltpu.SemaphoreType.DMA((3,))
        ],
        compiler_params=pltpu.CompilerParams(vmem_limit_bytes=SMALL_VMEM),
    )(here, *arrays)


def counted(condition):
    return jnp.sum(jnp.where(condition, 1.0, 0.0)).astype(jnp.int32)


def plan(frame_count, here, meta, sc, lines, starts, ends):
    n, _, double = meta.shape
    count = double // 2
    for i in range(n):
        lines[i : i + 1, :] = meta[i].astype(jnp.float32)[:1]
    dur, seg = lines[:, :count], lines[:, count:]
    rows = lax.broadcasted_iota(jnp.int32, (count, count), 0)
    cols = lax.broadcasted_iota(jnp.int32, (count, count), 1)
    upper = jnp.where(rows <= cols, 1.0, 0.0).astype(jnp.bfloat16)
    running = jnp.dot(dur.astype(jnp.bfloat16), upper, preferred_element_type=jnp.float32)
    sums = jnp.sum(dur, axis=1, keepdims=True)
    starts[...] = jnp.zeros_like(starts)
    ends[...] = jnp.zeros_like(ends)
    before = jnp.zeros((1, 1), jnp.float32)
    for r in range(n):
        ends[r : r + 1, :] = (running[r : r + 1, :] + before).astype(jnp.int32)
        before = before + sums[r : r + 1, :]
    done = ends[pl.ds(0, n), :]
    starts[pl.ds(0, n), :] = done - dur.astype(jnp.int32)
    half = KERNEL // 2
    frame0 = here * frame_count
    first = counted(done <= jnp.maximum(frame0 - half, 0))
    last = counted(done <= jnp.minimum(frame0 + frame_count + half, n * frame_count) - 1)
    base = lax.div(first, ALIGN) * ALIGN
    windows = lax.div(last - base + WIN, WIN)
    sc[0] = jnp.minimum(base, n * count - windows * WIN)
    sc[1] = windows
    sc[2] = frame0
    for v in range(SEGS + 1):
        sc[4 + v] = counted(seg < v)


def load_body(here, source, target, token, sems):
    token[...] = jnp.zeros_like(token)
    rows = source.shape[0] // LOADS
    copies = []
    for i in range(LOADS):
        part = pl.ds(i * rows, rows)
        copies.append(pltpu.make_async_copy(source.at[part], target.at[part], sems.at[i]))
    for copy in copies:
        copy.start()
    for copy in copies:
        copy.wait()


def load(here, array):
    return pl.pallas_call(
        load_body,
        out_shape=(
            pltpu.VMEM(array.shape, array.dtype), jax.ShapeDtypeStruct((8, 128), jnp.float32)
        ),
        in_specs=[pl.BlockSpec(memory_space=pltpu.SMEM), pl.BlockSpec(memory_space=pltpu.HBM)],
        out_specs=(pl.BlockSpec(memory_space=pltpu.VMEM),) * 2,
        scratch_shapes=[pltpu.SemaphoreType.DMA((LOADS,))],
        cost_estimate=pl.CostEstimate(
            flops=0, bytes_accessed=2 * array.size * array.dtype.itemsize, transcendentals=0
        ),
        compiler_params=pltpu.CompilerParams(vmem_limit_bytes=PROJECT_VMEM),
    )(here, pltpu.with_memory_space_constraint(array, pltpu.HBM))


def project_body(step, dy, outer, here, x0, x1, gain, w, *rest):
    ks, vs, xa, meta, token, hs, sem = rest[-7:]
    rows, width = x0.shape
    rows = rows - EXTRA
    slot = lax.rem(lax.div(here[0], 4) + outer - step, outer) * 2 + (lax.rem(lax.div(here[0], 2), 2) ^ dy)
    core = lax.rem(here[0], 2)
    copies = []
    for i, ref in enumerate((x0, x1)):
        start = pl.multiple_of(slot * 2 * rows + (core ^ i) * rows, rows)
        copies.append(
            pltpu.make_async_copy(ref.at[pl.ds(0, rows)], xa.at[pl.ds(start, rows)], sem.at[i])
        )
        ids = ref.at[pl.ds(rows, EXTRA), pl.ds(0, meta.shape[2])]
        copies.append(pltpu.make_async_copy(ids, meta.at[slot * 2 + (core ^ i)], sem.at[2 + i]))
    for copy in copies:
        copy.start()
    for copy in copies:
        copy.wait()
    pair = pl.ds(pl.multiple_of(slot * 2 * rows, 2 * rows), 2 * rows)
    token[...] = jnp.zeros_like(token)
    hs[...] = rows_normalized(xa[pair, :].astype(jnp.float32), gain[...]).astype(jnp.bfloat16)
    cols = 256
    for c in range(width, 2 * width, cols):
        k = jnp.dot(hs[...], w[:, c : c + cols], preferred_element_type=jnp.float32)
        ks[slot, :, c - width : c - width + cols] = k.astype(jnp.bfloat16)
    for c in range(2 * width, 3 * width, cols):
        v = jnp.dot(hs[...], w[:, c : c + cols], preferred_element_type=jnp.float32)
        vs[slot, c - 2 * width : c - 2 * width + cols, :] = v.astype(jnp.bfloat16).T


def project(step, dy, outer, here, blocks, gain, w_qkv, previous, after, units):
    rows, width = blocks[0].shape
    rows = rows - EXTRA
    pair = 2 * rows
    pairs = units // pair
    vmem = pl.BlockSpec(memory_space=pltpu.VMEM)
    any_spec = pl.BlockSpec(memory_space=pl.ANY)
    operands = [here, *blocks, gain, w_qkv]
    in_specs = [pl.BlockSpec(memory_space=pltpu.SMEM), any_spec, any_spec, vmem, vmem]
    in_specs += [any_spec] * len(after)
    operands += list(after)
    aliases = {}
    if previous is not None:
        aliases = {len(operands) + i: i for i in range(4)}
        in_specs += [any_spec] * 4
        operands += list(previous)
    return pl.pallas_call(
        functools.partial(project_body, step, dy, outer),
        out_shape=(
            pltpu.VMEM((pairs, pair, width), jnp.bfloat16),
            pltpu.VMEM((pairs, width, pair), jnp.bfloat16),
            pltpu.VMEM((units, width), jnp.bfloat16),
            pltpu.VMEM((units // rows, EXTRA, 2 * rows), jnp.bfloat16),
            jax.ShapeDtypeStruct((8, 128), jnp.float32),
        ),
        in_specs=in_specs,
        out_specs=(vmem,) * 5,
        scratch_shapes=[pltpu.VMEM((pair, width), jnp.bfloat16), pltpu.SemaphoreType.DMA((4,))],
        input_output_aliases=aliases,
        cost_estimate=pl.CostEstimate(
            flops=2 * pair * width * 2 * width,
            bytes_accessed=2 * (width * 2 * width + 4 * pair * width),
            transcendentals=0,
        ),
        compiler_params=pltpu.CompilerParams(vmem_limit_bytes=PROJECT_VMEM),
    )(*operands)


def frames_body(
    here, meta, gain, conv_b, conv_gain, xa, keys, values, w_qkv, w_out, w_proj, conv_w,
    out, wo, wp, cw, xw, qs, begun, bias, acc, acc_rest, tops, totals, turned, red,
    expanded, sc, lines, starts, ends, sems,
):
    width = w_out.shape[0]
    channels = w_proj.shape[1]
    head = width // HEADS
    deep = GROUP * head
    frames = out.shape[0]
    tile = keys.shape[1]
    half = KERNEL // 2
    scale = math.log2(math.e) / math.sqrt(head)

    load_o = pltpu.make_async_copy(w_out, wo, sems.at[1])
    load_p = pltpu.make_async_copy(w_proj, wp, sems.at[2])
    load_c = pltpu.make_async_copy(conv_w, cw, sems.at[3])
    load_o.start()
    load_p.start()
    load_c.start()

    plan(frames, here[0], meta, sc, lines, starts, ends)
    base, windows, frame0 = sc[0], sc[1], sc[2]

    def seg_start(v):
        return sc[4 + v]

    def window(w, carry):
        r0 = pl.multiple_of(base + w * WIN, ALIGN)
        load_x = pltpu.make_async_copy(xa.at[pl.ds(r0, WIN)], xw, sems.at[4])
        load_x.start()
        lo, hi = jnp.int32(0), jnp.int32(0)
        for v in range(SEGS):
            lo = jnp.where(r0 >= seg_start(v), seg_start(v), lo)
            hi = jnp.where(r0 + WIN - 1 >= seg_start(v), seg_start(v + 1), hi)
        t0 = lax.div(lo, tile)
        t1 = lax.div(hi + tile - 1, tile)

        load_x.wait()
        h = rows_normalized(xw[...].astype(jnp.float32), gain[...]).astype(jnp.bfloat16)
        q = jnp.dot(h, w_qkv[:, :width], preferred_element_type=jnp.float32).astype(jnp.bfloat16)
        owner = lax.broadcasted_iota(jnp.int32, (WIN, deep), 1) // head
        zero = jnp.zeros((WIN, deep), jnp.bfloat16)
        for g in range(HEADS // GROUP):
            part = q[:, g * deep : (g + 1) * deep]
            for j in range(GROUP):
                alone = jnp.where(owner == j, part, zero)
                qs[g, j * MAIN : (j + 1) * MAIN, :] = alone[:MAIN]
                start = GROUP * MAIN + j * REST
                qs[g, start : start + REST, :] = alone[MAIN:]
        acc[...] = jnp.zeros_like(acc)
        acc_rest[...] = jnp.zeros_like(acc_rest)
        tops[...] = jnp.full_like(tops, LOW)
        totals[...] = jnp.zeros_like(totals)

        lane = lax.broadcasted_iota(jnp.int32, (1, 2 * MAIN), 1)
        row = r0 + jnp.where(lane < MAIN, lane, MAIN + (lane - MAIN) % REST)
        row_lo = jnp.zeros_like(row)
        row_hi = jnp.zeros_like(row)
        for v in range(SEGS):
            row_lo = jnp.where(row >= seg_start(v), seg_start(v), row_lo)
            row_hi = jnp.where(row >= seg_start(v), seg_start(v + 1), row_hi)

        def scores(t, g):
            dims = slice(g * deep, (g + 1) * deep)
            return lax.dot_general(
                keys[t, :, dims], qs[g], (((1,), (1,)), ((), ())),
                preferred_element_type=jnp.float32,
            )

        begun[...] = scores(t0, 0)

        def key_step(t, c):
            key = t * tile + lax.broadcasted_iota(jnp.int32, (tile, 2 * MAIN), 0)
            bias[...] = jnp.where((key >= row_lo) & (key < row_hi), 0.0, MASKED)
            main = bias[:, :MAIN]
            mask = jnp.concatenate([main] * GROUP + [bias[:, MAIN:]], axis=1)
            groups = HEADS // GROUP

            ahead = begun[...]
            for g in range(groups):
                dims = slice(g * deep, (g + 1) * deep)
                s = ahead * scale + mask
                if g + 1 < groups:
                    ahead = scores(t, g + 1)
                else:
                    begun[...] = scores(jnp.minimum(t + 1, t1 - 1), 0)
                top = tops[g]
                new_top = jnp.maximum(top, jnp.max(s, axis=0, keepdims=True))
                expo = jnp.exp2(s - new_top)
                alpha = jnp.exp2(top - new_top)
                tops[g] = new_top
                totals[g] = totals[g] * alpha + jnp.sum(expo, axis=0, keepdims=True)
                expo = expo.astype(jnp.bfloat16)
                for j in range(GROUP):
                    lanes = slice(j * MAIN, (j + 1) * MAIN)
                    start = g * deep + j * head
                    acc[g, j] = acc[g, j] * alpha[:, lanes] + jnp.dot(
                        values[t, start : start + head, :], expo[:, lanes],
                        preferred_element_type=jnp.float32,
                    )
                acc_rest[g] = acc_rest[g] * alpha[:, GROUP * MAIN :] + jnp.dot(
                    values[t, dims, :], expo[:, GROUP * MAIN :],
                    preferred_element_type=jnp.float32,
                )
            return c

        lax.fori_loop(t0, t1, key_step, 0)

        for g in range(HEADS // GROUP):
            total = totals[g]
            total = jnp.where(total == 0.0, 1.0, total)
            for j in range(GROUP):
                start = g * deep + j * head
                lanes = slice(j * MAIN, (j + 1) * MAIN)
                turned[start : start + head, :MAIN] = acc[g, j] / total[:, lanes]
            rest = acc_rest[g] / total[:, GROUP * MAIN :]
            for j in range(GROUP):
                start = g * deep + j * head
                turned[start : start + head, MAIN:WIN] = rest[
                    j * head : (j + 1) * head, j * REST : (j + 1) * REST
                ]
        attended = turned[...].T[:WIN].astype(jnp.bfloat16)

        @pl.when(w == 0)
        def _():
            load_o.wait()
            load_p.wait()

        mixed = jnp.dot(attended, wo[...], preferred_element_type=jnp.float32) + xw[...].astype(
            jnp.float32
        )
        reduced = jnp.dot(
            mixed.astype(jnp.bfloat16), wp[...], preferred_element_type=jnp.float32
        ).astype(jnp.bfloat16)
        red[pl.ds(0, WIN), :] = reduced
        red[pl.ds(WIN, LANES - WIN), :] = jnp.zeros((LANES - WIN, channels), jnp.bfloat16)
        shape = (frames + 2 * HALO, LANES)
        frame = frame0 - HALO + lax.broadcasted_iota(jnp.int32, shape, 0)
        lanes = starts.shape[1]
        row0 = lax.div(r0, lanes)
        shift = 3 * lanes - lax.rem(r0, lanes)

        def cut(ref):
            line = jnp.concatenate([ref[pl.ds(row0 + i, 1), :] for i in range(3)], axis=1)
            line = pltpu.roll(jnp.broadcast_to(line, (8, 3 * lanes)), shift, 1)[:1, :LANES]
            return jnp.where(lax.broadcasted_iota(jnp.int32, (1, LANES), 1) < WIN, line, 0)

        pick = jnp.where((frame >= cut(starts)) & (frame < cut(ends)), 1.0, 0.0).astype(jnp.bfloat16)
        rows = jnp.dot(pick, red[...], preferred_element_type=jnp.float32)

        @pl.when(w == 0)
        def _():
            expanded[...] = rows

        @pl.when(w > 0)
        def _():
            expanded[...] += rows

        return carry

    lax.fori_loop(0, windows, window, 0)

    load_c.wait()
    block = 256
    for b in range(frames // block):
        conv = jnp.zeros((block, channels), jnp.float32) + conv_b[...]
        for tap in range(KERNEL):
            part = expanded[pl.ds(b * block + HALO - half + tap, block), :].astype(jnp.bfloat16)
            conv = conv + jnp.dot(part, cw[tap], preferred_element_type=jnp.float32)
        result = expanded[pl.ds(b * block + HALO, block), :] + rows_normalized(
            jnp.maximum(conv, 0.0), conv_gain[...]
        )
        out[pl.ds(b * block, block), :] = result.astype(jnp.bfloat16)


def frames_call(here, meta, gain, conv_b, conv_gain, xa, ks, vs, w_qkv, w_out, w_proj, conv_w, frames):
    _, width = xa.shape
    channels = w_proj.shape[1]
    head = width // HEADS
    hbm = pl.BlockSpec(memory_space=pltpu.HBM)
    vmem = pl.BlockSpec(memory_space=pltpu.VMEM)
    groups = HEADS // GROUP
    return pl.pallas_call(
        frames_body,
        out_shape=jax.ShapeDtypeStruct((frames, channels), jnp.bfloat16),
        in_specs=[pl.BlockSpec(memory_space=pltpu.SMEM)] + [vmem] * 8 + [hbm] * 3,
        out_specs=vmem,
        scratch_shapes=[
            pltpu.VMEM((width, width), jnp.bfloat16),
            pltpu.VMEM((width, channels), jnp.bfloat16),
            pltpu.VMEM((KERNEL, channels, channels), jnp.bfloat16),
            pltpu.VMEM((WIN, width), jnp.bfloat16),
            pltpu.VMEM((groups, STACK, GROUP * head), jnp.bfloat16),
            pltpu.VMEM((ks.shape[1], STACK), jnp.float32),
            pltpu.VMEM((ks.shape[1], 2 * MAIN), jnp.float32),
            pltpu.VMEM((groups, GROUP, head, MAIN), jnp.float32),
            pltpu.VMEM((groups, GROUP * head, GROUP * REST), jnp.float32),
            pltpu.VMEM((groups, 1, STACK), jnp.float32),
            pltpu.VMEM((groups, 1, STACK), jnp.float32),
            pltpu.VMEM((width, 2 * MAIN), jnp.float32),
            pltpu.VMEM((LANES, channels), jnp.bfloat16),
            pltpu.VMEM((frames + 2 * HALO, channels), jnp.float32),
            pltpu.SMEM((SEGS + 5,), jnp.int32),
            pltpu.VMEM((meta.shape[0], meta.shape[2]), jnp.float32),
            pltpu.VMEM((meta.shape[0] + 8, meta.shape[2] // 2), jnp.int32),
            pltpu.VMEM((meta.shape[0] + 8, meta.shape[2] // 2), jnp.int32),
            pltpu.SemaphoreType.DMA((5,)),
        ],
        compiler_params=pltpu.CompilerParams(vmem_limit_bytes=FRAMES_VMEM),
    )(here, meta, gain, conv_b, conv_gain, xa, ks, vs, w_qkv, w_out, w_proj, conv_w)


def local(units, durations, seg_ids, ln_gain, w_qkv, w_out, w_proj, conv_w, conv_b, conv_gain):
    n = lax.axis_size("seq")
    outer = n // 4
    here = lax.axis_index("seq")
    count = units.shape[0]
    total = n * count
    frame_count = DUR_MEAN * count

    def place(z, y, c):
        return (z * 2 + y) * 2 + c

    def pairs(step, dy, dc):
        return [
            (place(z, y, c), place((z + step) % outer, y ^ dy, c ^ dc))
            for z in range(outer)
            for y in range(2)
            for c in range(2)
        ]

    def send(value, step, dy=0, dc=0):
        return lax.ppermute(value, "seq", pairs(step, dy, dc))

    gain = ln_gain[None, :]
    w_out, w_proj, conv_w = [
        pltpu.with_memory_space_constraint(w, pltpu.HBM) for w in (w_out, w_proj, conv_w)
    ]
    where = here.reshape(1)

    def kernel(distance, dy, blocks, state, *after):
        *state, token = project(
            distance % outer, dy, outer, where, blocks, gain, w_qkv, state, after, total
        )
        return state, token

    w_qkv, token = load(where, w_qkv)
    far_up, far_down = outer // 2, (outer - 1) // 2

    def in_rounds(own, state, token):
        up = down = own
        arrived = [(0, own)]
        waiting = []
        for step in range(far_up + 1):
            following = []
            if step < far_up:
                up = send(up, 1)
                following.append((step + 1, up))
            if step < far_down:
                down = send(down, outer - 1)
                following.append((-(step + 1), down))
            for pair in waiting:
                state, token = kernel(*pair, state, token)
            if waiting and following:
                held = lax.optimization_barrier((token, *[block for _, block in arrived]))
                token = held[0]
                arrived = [(d, block) for (d, _), block in zip(arrived, held[1:])]
            sides = []
            for d, block in arrived:
                if step == far_up and step > 1:
                    across = send(waiting_up, 1)
                else:
                    across = send(block, 0, 1, 0)
                sides.append((d, block, across, send(block, 0, 0, 1)))
            for d, block, across, beside in sides:
                state, token = kernel(d, 0, (block, beside), state, token)
            if step == 0:
                ((d, _, across, _),) = sides
                token, across = lax.optimization_barrier((token, across))
                diagonal = send(across, 0, 0, 1)
                state, token = kernel(d, 1, (across, diagonal), state, token)
            halves = [across for _, _, across, _ in sides]
            if following:
                held = lax.optimization_barrier((token, *[block for _, block in following]))
                token = held[0]
                following = [(d, block) for (d, _), block in zip(following, held[1:])]
                up = following[0][1]
                down = following[1][1] if len(following) > 1 else None
            waiting = []
            for (d, _, _, _), across in zip(sides if step > 0 else (), halves):
                token, across = lax.optimization_barrier((token, across))
                waiting.append((d, 1, (across, send(across, 0, 0, 1))))
            waiting_up = sides[0][2]
            arrived = following
        for pair in waiting:
            state, token = kernel(*pair, state, token)
        return state

    def four_planes(own, state, token):
        def tie(token, *blocks):
            return lax.optimization_barrier((token, *blocks))

        up = send(own, 1)
        across = send(own, 0, 1, 0)
        beside = send(own, 0, 0, 1)
        token, later = tie(token, own)
        down = send(later, outer - 1)
        state, token = kernel(0, 0, (own, beside), state, token)
        token, up = tie(token, up)
        far = send(up, 1)
        up_across = send(up, 0, 1, 0)
        up_beside = send(up, 0, 0, 1)
        token, across = tie(token, across)
        diagonal = send(across, 0, 0, 1)
        state, token = kernel(1, 0, (up, up_beside), state, token)
        state, token = kernel(0, 1, (across, diagonal), state, token)
        token, down = tie(token, down)
        down_across = send(down, 0, 1, 0)
        down_beside = send(down, 0, 0, 1)
        token, up_across = tie(token, up_across)
        far_across = send(up_across, 1)
        up_diagonal = send(up_across, 0, 0, 1)
        far_beside = send(far, 0, 0, 1)
        state, token = kernel(-1, 0, (down, down_beside), state, token)
        state, token = kernel(1, 1, (up_across, up_diagonal), state, token)
        state, token = kernel(2, 0, (far, far_beside), state, token)
        token, down_across = tie(token, down_across)
        down_diagonal = send(down_across, 0, 0, 1)
        far_diagonal = send(far_across, 0, 0, 1)
        state, token = kernel(-1, 1, (down_across, down_diagonal), state, token)
        state, token = kernel(2, 1, (far_across, far_diagonal), state, token)
        return state

    own = pack(where, units, durations[None, :], seg_ids[None, :])
    state = (four_planes if outer == 4 else in_rounds)(own, None, token)
    ks, vs, xa, meta = state
    return frames_call(
        where, meta, gain, conv_b[None, :], conv_gain[None, :], xa, ks, vs, w_qkv, w_out, w_proj,
        conv_w, frame_count,
    )


def solution(mesh):
    split = P(("grp", "seq"))
    in_specs = (P(("grp", "seq"), None), split, split) + (P(),) * 7
    return jax.shard_map(
        local, mesh=mesh, in_specs=in_specs, out_specs=P(("grp", "seq"), None), check_vma=False
    )
```

```python
import functools
import math

import jax
import jax.numpy as jnp
from jax import lax
from jax.experimental import pallas as pl
from jax.experimental.pallas import tpu as pltpu
from jax.sharding import PartitionSpec as P


HEADS = 16
KERNEL = 5
SEGS = 8
DUR_MEAN = 6
EPS = 1e-05

MAIN = 128
REST = 32
WIN = MAIN + REST
GROUP = 4
STACK = GROUP * WIN
ALIGN = 8
LANES = 256
HALO = 8
LOW = -1e30
MASKED = -2e30
LOADS = 8
SMALL_VMEM = 4 << 20
EXTRA = 8
PROJECT_VMEM = 6 << 20
FRAMES_VMEM = 24 << 20


def rows_normalized(values, gain):
    mean = jnp.mean(values, axis=-1, keepdims=True)
    centred = values - mean
    variance = jnp.mean(centred * centred, axis=-1, keepdims=True)
    return centred * lax.rsqrt(variance + EPS) * gain


def pack_body(here, units, dur, seg, out, ids, sems):
    rows, width = units.shape
    count = dur.shape[1]
    copies = [
        pltpu.make_async_copy(dur, ids.at[:, pl.ds(0, count)], sems.at[0]),
        pltpu.make_async_copy(seg, ids.at[:, pl.ds(count, count)], sems.at[1]),
        pltpu.make_async_copy(units, out.at[pl.ds(0, rows)], sems.at[2]),
    ]
    for copy in copies:
        copy.start()
    out[pl.ds(rows, EXTRA), :] = jnp.zeros((EXTRA, width), jnp.bfloat16)
    copies[0].wait()
    copies[1].wait()
    line = ids[...].astype(jnp.float32).astype(jnp.bfloat16)
    out[pl.ds(rows, EXTRA), : 2 * count] = jnp.broadcast_to(line, (EXTRA, 2 * count))
    copies[2].wait()


def pack(here, units, dur, seg):
    rows, width = units.shape
    hbm = pl.BlockSpec(memory_space=pltpu.HBM)
    arrays = [pltpu.with_memory_space_constraint(array, pltpu.HBM) for array in (units, dur, seg)]
    return pl.pallas_call(
        pack_body,
        out_shape=jax.ShapeDtypeStruct((rows + EXTRA, width), units.dtype),
        in_specs=[pl.BlockSpec(memory_space=pltpu.SMEM), hbm, hbm, hbm],
        out_specs=pl.BlockSpec(memory_space=pltpu.VMEM),
        scratch_shapes=[
            pltpu.VMEM((1, 2 * dur.shape[1]), jnp.int32), pltpu.SemaphoreType.DMA((3,))
        ],
        compiler_params=pltpu.CompilerParams(vmem_limit_bytes=SMALL_VMEM),
    )(here, *arrays)


def counted(condition):
    return jnp.sum(jnp.where(condition, 1.0, 0.0)).astype(jnp.int32)


def plan(frame_count, here, meta, sc, lines, starts, ends):
    n, _, double = meta.shape
    count = double // 2
    for i in range(n):
        lines[i : i + 1, :] = meta[i].astype(jnp.float32)[:1]
    dur, seg = lines[:, :count], lines[:, count:]
    rows = lax.broadcasted_iota(jnp.int32, (count, count), 0)
    cols = lax.broadcasted_iota(jnp.int32, (count, count), 1)
    upper = jnp.where(rows <= cols, 1.0, 0.0).astype(jnp.bfloat16)
    running = jnp.dot(dur.astype(jnp.bfloat16), upper, preferred_element_type=jnp.float32)
    sums = jnp.sum(dur, axis=1, keepdims=True)
    starts[...] = jnp.zeros_like(starts)
    ends[...] = jnp.zeros_like(ends)
    before = jnp.zeros((1, 1), jnp.float32)
    for r in range(n):
        ends[r : r + 1, :] = (running[r : r + 1, :] + before).astype(jnp.int32)
        before = before + sums[r : r + 1, :]
    done = ends[pl.ds(0, n), :]
    starts[pl.ds(0, n), :] = done - dur.astype(jnp.int32)
    half = KERNEL // 2
    frame0 = here * frame_count
    first = counted(done <= jnp.maximum(frame0 - half, 0))
    last = counted(done <= jnp.minimum(frame0 + frame_count + half, n * frame_count) - 1)
    base = lax.div(first, ALIGN) * ALIGN
    windows = lax.div(last - base + WIN, WIN)
    sc[0] = jnp.minimum(base, n * count - windows * WIN)
    sc[1] = windows
    sc[2] = frame0
    for v in range(SEGS + 1):
        sc[4 + v] = counted(seg < v)


def load_body(here, source, target, token, sems):
    token[...] = jnp.zeros_like(token)
    rows = source.shape[0] // LOADS
    copies = []
    for i in range(LOADS):
        part = pl.ds(i * rows, rows)
        copies.append(pltpu.make_async_copy(source.at[part], target.at[part], sems.at[i]))
    for copy in copies:
        copy.start()
    for copy in copies:
        copy.wait()


def load(here, array):
    return pl.pallas_call(
        load_body,
        out_shape=(
            pltpu.VMEM(array.shape, array.dtype), jax.ShapeDtypeStruct((8, 128), jnp.float32)
        ),
        in_specs=[pl.BlockSpec(memory_space=pltpu.SMEM), pl.BlockSpec(memory_space=pltpu.HBM)],
        out_specs=(pl.BlockSpec(memory_space=pltpu.VMEM),) * 2,
        scratch_shapes=[pltpu.SemaphoreType.DMA((LOADS,))],
        cost_estimate=pl.CostEstimate(
            flops=0, bytes_accessed=2 * array.size * array.dtype.itemsize, transcendentals=0
        ),
        compiler_params=pltpu.CompilerParams(vmem_limit_bytes=PROJECT_VMEM),
    )(here, pltpu.with_memory_space_constraint(array, pltpu.HBM))


def project_body(step, dy, outer, here, x0, x1, gain, w, *rest):
    ks, vs, xa, meta, token, hs, sem = rest[-7:]
    rows, width = x0.shape
    rows = rows - EXTRA
    slot = lax.rem(lax.div(here[0], 4) + outer - step, outer) * 2 + (lax.rem(lax.div(here[0], 2), 2) ^ dy)
    core = lax.rem(here[0], 2)
    copies = []
    for i, ref in enumerate((x0, x1)):
        start = pl.multiple_of(slot * 2 * rows + (core ^ i) * rows, rows)
        copies.append(
            pltpu.make_async_copy(ref.at[pl.ds(0, rows)], xa.at[pl.ds(start, rows)], sem.at[i])
        )
        ids = ref.at[pl.ds(rows, EXTRA), pl.ds(0, meta.shape[2])]
        copies.append(pltpu.make_async_copy(ids, meta.at[slot * 2 + (core ^ i)], sem.at[2 + i]))
    for copy in copies:
        copy.start()
    for copy in copies:
        copy.wait()
    pair = pl.ds(pl.multiple_of(slot * 2 * rows, 2 * rows), 2 * rows)
    token[...] = jnp.zeros_like(token)
    hs[...] = rows_normalized(xa[pair, :].astype(jnp.float32), gain[...]).astype(jnp.bfloat16)
    cols = 256
    for c in range(width, 2 * width, cols):
        k = jnp.dot(hs[...], w[:, c : c + cols], preferred_element_type=jnp.float32)
        ks[slot, :, c - width : c - width + cols] = k.astype(jnp.bfloat16)
    for c in range(2 * width, 3 * width, cols):
        v = jnp.dot(hs[...], w[:, c : c + cols], preferred_element_type=jnp.float32)
        vs[slot, c - 2 * width : c - 2 * width + cols, :] = v.astype(jnp.bfloat16).T


def project(step, dy, outer, here, blocks, gain, w_qkv, previous, after, units):
    rows, width = blocks[0].shape
    rows = rows - EXTRA
    pair = 2 * rows
    pairs = units // pair
    vmem = pl.BlockSpec(memory_space=pltpu.VMEM)
    any_spec = pl.BlockSpec(memory_space=pl.ANY)
    operands = [here, *blocks, gain, w_qkv]
    in_specs = [pl.BlockSpec(memory_space=pltpu.SMEM), any_spec, any_spec, vmem, vmem]
    in_specs += [any_spec] * len(after)
    operands += list(after)
    aliases = {}
    if previous is not None:
        aliases = {len(operands) + i: i for i in range(4)}
        in_specs += [any_spec] * 4
        operands += list(previous)
    return pl.pallas_call(
        functools.partial(project_body, step, dy, outer),
        out_shape=(
            pltpu.VMEM((pairs, pair, width), jnp.bfloat16),
            pltpu.VMEM((pairs, width, pair), jnp.bfloat16),
            pltpu.VMEM((units, width), jnp.bfloat16),
            pltpu.VMEM((units // rows, EXTRA, 2 * rows), jnp.bfloat16),
            jax.ShapeDtypeStruct((8, 128), jnp.float32),
        ),
        in_specs=in_specs,
        out_specs=(vmem,) * 5,
        scratch_shapes=[pltpu.VMEM((pair, width), jnp.bfloat16), pltpu.SemaphoreType.DMA((4,))],
        input_output_aliases=aliases,
        cost_estimate=pl.CostEstimate(
            flops=2 * pair * width * 2 * width,
            bytes_accessed=2 * (width * 2 * width + 4 * pair * width),
            transcendentals=0,
        ),
        compiler_params=pltpu.CompilerParams(vmem_limit_bytes=PROJECT_VMEM),
    )(*operands)


def frames_body(
    here, meta, gain, conv_b, conv_gain, xa, keys, values, w_qkv, w_out, w_proj, conv_w,
    out, wo, wp, cw, xw, qs, begun, bias, acc, acc_rest, tops, totals, turned, red,
    expanded, sc, lines, starts, ends, sems,
):
    width = w_out.shape[0]
    channels = w_proj.shape[1]
    head = width // HEADS
    deep = GROUP * head
    frames = out.shape[0]
    tile = keys.shape[1]
    half = KERNEL // 2
    scale = math.log2(math.e) / math.sqrt(head)

    load_o = pltpu.make_async_copy(w_out, wo, sems.at[1])
    load_p = pltpu.make_async_copy(w_proj, wp, sems.at[2])
    load_c = pltpu.make_async_copy(conv_w, cw, sems.at[3])
    load_o.start()
    load_p.start()
    load_c.start()

    plan(frames, here[0], meta, sc, lines, starts, ends)
    base, windows, frame0 = sc[0], sc[1], sc[2]

    def seg_start(v):
        return sc[4 + v]

    def window(w, carry):
        r0 = pl.multiple_of(base + w * WIN, ALIGN)
        load_x = pltpu.make_async_copy(xa.at[pl.ds(r0, WIN)], xw, sems.at[4])
        load_x.start()
        lo, hi = jnp.int32(0), jnp.int32(0)
        for v in range(SEGS):
            lo = jnp.where(r0 >= seg_start(v), seg_start(v), lo)
            hi = jnp.where(r0 + WIN - 1 >= seg_start(v), seg_start(v + 1), hi)
        t0 = lax.div(lo, tile)
        t1 = lax.div(hi + tile - 1, tile)

        load_x.wait()
        h = rows_normalized(xw[...].astype(jnp.float32), gain[...]).astype(jnp.bfloat16)
        q = jnp.dot(h, w_qkv[:, :width], preferred_element_type=jnp.float32).astype(jnp.bfloat16)
        owner = lax.broadcasted_iota(jnp.int32, (WIN, deep), 1) // head
        zero = jnp.zeros((WIN, deep), jnp.bfloat16)
        for g in range(HEADS // GROUP):
            part = q[:, g * deep : (g + 1) * deep]
            for j in range(GROUP):
                alone = jnp.where(owner == j, part, zero)
                qs[g, j * MAIN : (j + 1) * MAIN, :] = alone[:MAIN]
                start = GROUP * MAIN + j * REST
                qs[g, start : start + REST, :] = alone[MAIN:]
        acc[...] = jnp.zeros_like(acc)
        acc_rest[...] = jnp.zeros_like(acc_rest)
        tops[...] = jnp.full_like(tops, LOW)
        totals[...] = jnp.zeros_like(totals)

        lane = lax.broadcasted_iota(jnp.int32, (1, 2 * MAIN), 1)
        row = r0 + jnp.where(lane < MAIN, lane, MAIN + (lane - MAIN) % REST)
        row_lo = jnp.zeros_like(row)
        row_hi = jnp.zeros_like(row)
        for v in range(SEGS):
            row_lo = jnp.where(row >= seg_start(v), seg_start(v), row_lo)
            row_hi = jnp.where(row >= seg_start(v), seg_start(v + 1), row_hi)

        def scores(t, g):
            dims = slice(g * deep, (g + 1) * deep)
            return lax.dot_general(
                keys[t, :, dims], qs[g], (((1,), (1,)), ((), ())),
                preferred_element_type=jnp.float32,
            )

        begun[...] = scores(t0, 0)

        def key_step(t, c):
            key = t * tile + lax.broadcasted_iota(jnp.int32, (tile, 2 * MAIN), 0)
            bias[...] = jnp.where((key >= row_lo) & (key < row_hi), 0.0, MASKED)
            groups = HEADS // GROUP

            ahead = begun[...]
            for g in range(groups):
                dims = slice(g * deep, (g + 1) * deep)
                now = ahead
                if g + 1 < groups:
                    ahead = scores(t, g + 1)
                else:
                    begun[...] = scores(jnp.minimum(t + 1, t1 - 1), 0)
                for j in range(GROUP + 1):
                    lanes = slice(j * MAIN, (j + 1) * MAIN)
                    s = now[:, lanes] * scale + (bias[:, :MAIN] if j < GROUP else bias[:, MAIN:])
                    top = tops[g][:, lanes]
                    new_top = jnp.maximum(top, jnp.max(s, axis=0, keepdims=True))
                    expo = jnp.exp2(s - new_top)
                    alpha = jnp.exp2(top - new_top)
                    tops[g, :, lanes] = new_top
                    totals[g, :, lanes] = totals[g][:, lanes] * alpha + jnp.sum(expo, axis=0, keepdims=True)
                    expo = expo.astype(jnp.bfloat16)
                    if j < GROUP:
                        start = g * deep + j * head
                        acc[g, j] = acc[g, j] * alpha + jnp.dot(
                            values[t, start : start + head, :], expo, preferred_element_type=jnp.float32
                        )
                    else:
                        acc_rest[g] = acc_rest[g] * alpha + jnp.dot(
                            values[t, dims, :], expo, preferred_element_type=jnp.float32
                        )
            return c

        lax.fori_loop(t0, t1, key_step, 0)

        for g in range(HEADS // GROUP):
            total = totals[g]
            total = jnp.where(total == 0.0, 1.0, total)
            for j in range(GROUP):
                start = g * deep + j * head
                lanes = slice(j * MAIN, (j + 1) * MAIN)
                turned[start : start + head, :MAIN] = acc[g, j] / total[:, lanes]
            rest = acc_rest[g] / total[:, GROUP * MAIN :]
            for j in range(GROUP):
                start = g * deep + j * head
                turned[start : start + head, MAIN:WIN] = rest[
                    j * head : (j + 1) * head, j * REST : (j + 1) * REST
                ]
        attended = turned[...].T[:WIN].astype(jnp.bfloat16)

        @pl.when(w == 0)
        def _():
            load_o.wait()
            load_p.wait()

        mixed = jnp.dot(attended, wo[...], preferred_element_type=jnp.float32) + xw[...].astype(
            jnp.float32
        )
        reduced = jnp.dot(
            mixed.astype(jnp.bfloat16), wp[...], preferred_element_type=jnp.float32
        ).astype(jnp.bfloat16)
        red[pl.ds(0, WIN), :] = reduced
        red[pl.ds(WIN, LANES - WIN), :] = jnp.zeros((LANES - WIN, channels), jnp.bfloat16)
        shape = (frames + 2 * HALO, LANES)
        frame = frame0 - HALO + lax.broadcasted_iota(jnp.int32, shape, 0)
        lanes = starts.shape[1]
        row0 = lax.div(r0, lanes)
        shift = 3 * lanes - lax.rem(r0, lanes)

        def cut(ref):
            line = jnp.concatenate([ref[pl.ds(row0 + i, 1), :] for i in range(3)], axis=1)
            line = pltpu.roll(jnp.broadcast_to(line, (8, 3 * lanes)), shift, 1)[:1, :LANES]
            return jnp.where(lax.broadcasted_iota(jnp.int32, (1, LANES), 1) < WIN, line, 0)

        pick = jnp.where((frame >= cut(starts)) & (frame < cut(ends)), 1.0, 0.0).astype(jnp.bfloat16)
        rows = jnp.dot(pick, red[...], preferred_element_type=jnp.float32)

        @pl.when(w == 0)
        def _():
            expanded[...] = rows

        @pl.when(w > 0)
        def _():
            expanded[...] += rows

        return carry

    lax.fori_loop(0, windows, window, 0)

    load_c.wait()
    block = 256
    for b in range(frames // block):
        conv = jnp.zeros((block, channels), jnp.float32) + conv_b[...]
        for tap in range(KERNEL):
            part = expanded[pl.ds(b * block + HALO - half + tap, block), :].astype(jnp.bfloat16)
            conv = conv + jnp.dot(part, cw[tap], preferred_element_type=jnp.float32)
        result = expanded[pl.ds(b * block + HALO, block), :] + rows_normalized(
            jnp.maximum(conv, 0.0), conv_gain[...]
        )
        out[pl.ds(b * block, block), :] = result.astype(jnp.bfloat16)


def frames_call(here, meta, gain, conv_b, conv_gain, xa, ks, vs, w_qkv, w_out, w_proj, conv_w, frames):
    _, width = xa.shape
    channels = w_proj.shape[1]
    head = width // HEADS
    hbm = pl.BlockSpec(memory_space=pltpu.HBM)
    vmem = pl.BlockSpec(memory_space=pltpu.VMEM)
    groups = HEADS // GROUP
    return pl.pallas_call(
        frames_body,
        out_shape=jax.ShapeDtypeStruct((frames, channels), jnp.bfloat16),
        in_specs=[pl.BlockSpec(memory_space=pltpu.SMEM)] + [vmem] * 8 + [hbm] * 3,
        out_specs=vmem,
        scratch_shapes=[
            pltpu.VMEM((width, width), jnp.bfloat16),
            pltpu.VMEM((width, channels), jnp.bfloat16),
            pltpu.VMEM((KERNEL, channels, channels), jnp.bfloat16),
            pltpu.VMEM((WIN, width), jnp.bfloat16),
            pltpu.VMEM((groups, STACK, GROUP * head), jnp.bfloat16),
            pltpu.VMEM((ks.shape[1], STACK), jnp.float32),
            pltpu.VMEM((ks.shape[1], 2 * MAIN), jnp.float32),
            pltpu.VMEM((groups, GROUP, head, MAIN), jnp.float32),
            pltpu.VMEM((groups, GROUP * head, GROUP * REST), jnp.float32),
            pltpu.VMEM((groups, 1, STACK), jnp.float32),
            pltpu.VMEM((groups, 1, STACK), jnp.float32),
            pltpu.VMEM((width, 2 * MAIN), jnp.float32),
            pltpu.VMEM((LANES, channels), jnp.bfloat16),
            pltpu.VMEM((frames + 2 * HALO, channels), jnp.float32),
            pltpu.SMEM((SEGS + 5,), jnp.int32),
            pltpu.VMEM((meta.shape[0], meta.shape[2]), jnp.float32),
            pltpu.VMEM((meta.shape[0] + 8, meta.shape[2] // 2), jnp.int32),
            pltpu.VMEM((meta.shape[0] + 8, meta.shape[2] // 2), jnp.int32),
            pltpu.SemaphoreType.DMA((5,)),
        ],
        compiler_params=pltpu.CompilerParams(vmem_limit_bytes=FRAMES_VMEM),
    )(here, meta, gain, conv_b, conv_gain, xa, ks, vs, w_qkv, w_out, w_proj, conv_w)


def local(units, durations, seg_ids, ln_gain, w_qkv, w_out, w_proj, conv_w, conv_b, conv_gain):
    n = lax.axis_size("seq")
    outer = n // 4
    here = lax.axis_index("seq")
    count = units.shape[0]
    total = n * count
    frame_count = DUR_MEAN * count

    def place(z, y, c):
        return (z * 2 + y) * 2 + c

    def pairs(step, dy, dc):
        return [
            (place(z, y, c), place((z + step) % outer, y ^ dy, c ^ dc))
            for z in range(outer)
            for y in range(2)
            for c in range(2)
        ]

    def send(value, step, dy=0, dc=0):
        return lax.ppermute(value, "seq", pairs(step, dy, dc))

    gain = ln_gain[None, :]
    w_out, w_proj, conv_w = [
        pltpu.with_memory_space_constraint(w, pltpu.HBM) for w in (w_out, w_proj, conv_w)
    ]
    where = here.reshape(1)

    def kernel(distance, dy, blocks, state, *after):
        *state, token = project(
            distance % outer, dy, outer, where, blocks, gain, w_qkv, state, after, total
        )
        return state, token

    w_qkv, token = load(where, w_qkv)
    far_up, far_down = outer // 2, (outer - 1) // 2

    def in_rounds(own, state, token):
        up = down = own
        arrived = [(0, own)]
        waiting = []
        for step in range(far_up + 1):
            following = []
            if step < far_up:
                up = send(up, 1)
                following.append((step + 1, up))
            if step < far_down:
                down = send(down, outer - 1)
                following.append((-(step + 1), down))
            for pair in waiting:
                state, token = kernel(*pair, state, token)
            if waiting and following:
                held = lax.optimization_barrier((token, *[block for _, block in arrived]))
                token = held[0]
                arrived = [(d, block) for (d, _), block in zip(arrived, held[1:])]
            sides = []
            for d, block in arrived:
                if step == far_up and step > 1:
                    across = send(waiting_up, 1)
                else:
                    across = send(block, 0, 1, 0)
                sides.append((d, block, across, send(block, 0, 0, 1)))
            for d, block, across, beside in sides:
                state, token = kernel(d, 0, (block, beside), state, token)
            if step == 0:
                ((d, _, across, _),) = sides
                token, across = lax.optimization_barrier((token, across))
                diagonal = send(across, 0, 0, 1)
                state, token = kernel(d, 1, (across, diagonal), state, token)
            halves = [across for _, _, across, _ in sides]
            if following:
                held = lax.optimization_barrier((token, *[block for _, block in following]))
                token = held[0]
                following = [(d, block) for (d, _), block in zip(following, held[1:])]
                up = following[0][1]
                down = following[1][1] if len(following) > 1 else None
            waiting = []
            for (d, _, _, _), across in zip(sides if step > 0 else (), halves):
                token, across = lax.optimization_barrier((token, across))
                waiting.append((d, 1, (across, send(across, 0, 0, 1))))
            waiting_up = sides[0][2]
            arrived = following
        for pair in waiting:
            state, token = kernel(*pair, state, token)
        return state

    def four_planes(own, state, token):
        def tie(token, *blocks):
            return lax.optimization_barrier((token, *blocks))

        up = send(own, 1)
        across = send(own, 0, 1, 0)
        beside = send(own, 0, 0, 1)
        token, later = tie(token, own)
        down = send(later, outer - 1)
        state, token = kernel(0, 0, (own, beside), state, token)
        token, up = tie(token, up)
        far = send(up, 1)
        up_across = send(up, 0, 1, 0)
        up_beside = send(up, 0, 0, 1)
        token, across = tie(token, across)
        diagonal = send(across, 0, 0, 1)
        state, token = kernel(1, 0, (up, up_beside), state, token)
        state, token = kernel(0, 1, (across, diagonal), state, token)
        token, down = tie(token, down)
        down_across = send(down, 0, 1, 0)
        down_beside = send(down, 0, 0, 1)
        token, up_across = tie(token, up_across)
        far_across = send(up_across, 1)
        up_diagonal = send(up_across, 0, 0, 1)
        state, token = kernel(-1, 0, (down, down_beside), state, token)
        state, token = kernel(1, 1, (up_across, up_diagonal), state, token)
        token, far = tie(token, far)
        far_beside = send(far, 0, 0, 1)
        token, down_across = tie(token, down_across)
        down_diagonal = send(down_across, 0, 0, 1)
        state, token = kernel(2, 0, (far, far_beside), state, token)
        state, token = kernel(-1, 1, (down_across, down_diagonal), state, token)
        token, far_across = tie(token, far_across)
        far_diagonal = send(far_across, 0, 0, 1)
        state, token = kernel(2, 1, (far_across, far_diagonal), state, token)
        return state

    own = pack(where, units, durations[None, :], seg_ids[None, :])
    state = (four_planes if outer == 4 else in_rounds)(own, None, token)
    ks, vs, xa, meta = state
    return frames_call(
        where, meta, gain, conv_b[None, :], conv_gain[None, :], xa, ks, vs, w_qkv, w_out, w_proj,
        conv_w, frame_count,
    )


def solution(mesh):
    split = P(("grp", "seq"))
    in_specs = (P(("grp", "seq"), None), split, split) + (P(),) * 7
    return jax.shard_map(
        local, mesh=mesh, in_specs=in_specs, out_specs=P(("grp", "seq"), None), check_vma=False
    )
```

```python
import functools
import math

import jax
import jax.numpy as jnp
from jax import lax
from jax.experimental import pallas as pl
from jax.experimental.pallas import tpu as pltpu
from jax.sharding import PartitionSpec as P


HEADS = 16
KERNEL = 5
SEGS = 8
DUR_MEAN = 6
EPS = 1e-05

MAIN = 128
REST = 32
WIN = MAIN + REST
GROUP = 4
STACK = GROUP * WIN
ALIGN = 8
LANES = 256
HALO = 8
OUT_ROWS = 256
LOW = -1e30
MASKED = -2e30
LOADS = 8
PARTS = 4
SMALL_VMEM = 4 << 20
EXTRA = 8
PROJECT_VMEM = 6 << 20
FRAMES_VMEM = 24 << 20


def rows_normalized(values, gain):
    mean = jnp.mean(values, axis=-1, keepdims=True)
    centred = values - mean
    variance = jnp.mean(centred * centred, axis=-1, keepdims=True)
    return centred * lax.rsqrt(variance + EPS) * gain


def pack_body(here, units, dur, seg, out, ids, sems):
    rows, width = units.shape
    count = dur.shape[1]
    copies = [
        pltpu.make_async_copy(dur, ids.at[:, pl.ds(0, count)], sems.at[0]),
        pltpu.make_async_copy(seg, ids.at[:, pl.ds(count, count)], sems.at[1]),
    ]
    part = rows // PARTS
    for i in range(PARTS):
        own = pl.ds(i * part, part)
        copies.append(pltpu.make_async_copy(units.at[own], out.at[own], sems.at[2 + i]))
    for copy in copies:
        copy.start()
    out[pl.ds(rows, EXTRA), :] = jnp.zeros((EXTRA, width), jnp.bfloat16)
    copies[0].wait()
    copies[1].wait()
    line = ids[...].astype(jnp.float32).astype(jnp.bfloat16)
    out[pl.ds(rows, EXTRA), : 2 * count] = jnp.broadcast_to(line, (EXTRA, 2 * count))
    for copy in copies[2:]:
        copy.wait()


def pack(here, units, dur, seg):
    rows, width = units.shape
    hbm = pl.BlockSpec(memory_space=pltpu.HBM)
    arrays = [pltpu.with_memory_space_constraint(array, pltpu.HBM) for array in (units, dur, seg)]
    return pl.pallas_call(
        pack_body,
        out_shape=jax.ShapeDtypeStruct((rows + EXTRA, width), units.dtype),
        in_specs=[pl.BlockSpec(memory_space=pltpu.SMEM), hbm, hbm, hbm],
        out_specs=pl.BlockSpec(memory_space=pltpu.VMEM),
        scratch_shapes=[
            pltpu.VMEM((1, 2 * dur.shape[1]), jnp.int32), pltpu.SemaphoreType.DMA((2 + PARTS,))
        ],
        compiler_params=pltpu.CompilerParams(vmem_limit_bytes=SMALL_VMEM),
    )(here, *arrays)


def counted(condition):
    return jnp.sum(jnp.where(condition, 1.0, 0.0)).astype(jnp.int32)


def plan(frame_count, here, meta, sc, lines, starts, ends):
    n, _, double = meta.shape
    count = double // 2
    for i in range(n):
        lines[i : i + 1, :] = meta[i].astype(jnp.float32)[:1]
    dur, seg = lines[:, :count], lines[:, count:]
    rows = lax.broadcasted_iota(jnp.int32, (count, count), 0)
    cols = lax.broadcasted_iota(jnp.int32, (count, count), 1)
    upper = jnp.where(rows <= cols, 1.0, 0.0).astype(jnp.bfloat16)
    running = jnp.dot(dur.astype(jnp.bfloat16), upper, preferred_element_type=jnp.float32)
    sums = jnp.sum(dur, axis=1, keepdims=True)
    starts[...] = jnp.zeros_like(starts)
    ends[...] = jnp.zeros_like(ends)
    before = jnp.zeros((1, 1), jnp.float32)
    for r in range(n):
        ends[r : r + 1, :] = (running[r : r + 1, :] + before).astype(jnp.int32)
        before = before + sums[r : r + 1, :]
    done = ends[pl.ds(0, n), :]
    starts[pl.ds(0, n), :] = done - dur.astype(jnp.int32)
    half = KERNEL // 2
    frame0 = here * frame_count
    first = counted(done <= jnp.maximum(frame0 - half, 0))
    last = counted(done <= jnp.minimum(frame0 + frame_count + half, n * frame_count) - 1)
    base = lax.div(first, ALIGN) * ALIGN
    windows = lax.div(last - base + WIN, WIN)
    sc[0] = jnp.minimum(base, n * count - windows * WIN)
    sc[1] = windows
    sc[2] = frame0
    for v in range(SEGS + 1):
        sc[4 + v] = counted(seg < v)


def load_body(here, source, target, token, sems):
    token[...] = jnp.zeros_like(token)
    rows = source.shape[0] // LOADS
    copies = []
    for i in range(LOADS):
        part = pl.ds(i * rows, rows)
        copies.append(pltpu.make_async_copy(source.at[part], target.at[part], sems.at[i]))
    for copy in copies:
        copy.start()
    for copy in copies:
        copy.wait()


def load(here, array):
    return pl.pallas_call(
        load_body,
        out_shape=(
            pltpu.VMEM(array.shape, array.dtype), jax.ShapeDtypeStruct((8, 128), jnp.float32)
        ),
        in_specs=[pl.BlockSpec(memory_space=pltpu.SMEM), pl.BlockSpec(memory_space=pltpu.HBM)],
        out_specs=(pl.BlockSpec(memory_space=pltpu.VMEM),) * 2,
        scratch_shapes=[pltpu.SemaphoreType.DMA((LOADS,))],
        cost_estimate=pl.CostEstimate(
            flops=0, bytes_accessed=2 * array.size * array.dtype.itemsize, transcendentals=0
        ),
        compiler_params=pltpu.CompilerParams(vmem_limit_bytes=PROJECT_VMEM),
    )(here, pltpu.with_memory_space_constraint(array, pltpu.HBM))


def project_body(step, dy, outer, here, x0, x1, gain, w, *rest):
    ks, vs, xa, meta, token, hs, sem = rest[-7:]
    rows, width = x0.shape
    rows = rows - EXTRA
    slot = lax.rem(lax.div(here[0], 4) + outer - step, outer) * 2 + (lax.rem(lax.div(here[0], 2), 2) ^ dy)
    core = lax.rem(here[0], 2)
    copies = []
    for i, ref in enumerate((x0, x1)):
        start = pl.multiple_of(slot * 2 * rows + (core ^ i) * rows, rows)
        copies.append(
            pltpu.make_async_copy(ref.at[pl.ds(0, rows)], xa.at[pl.ds(start, rows)], sem.at[i])
        )
        ids = ref.at[pl.ds(rows, EXTRA), pl.ds(0, meta.shape[2])]
        copies.append(pltpu.make_async_copy(ids, meta.at[slot * 2 + (core ^ i)], sem.at[2 + i]))
    for copy in copies:
        copy.start()
    for copy in copies:
        copy.wait()
    pair = pl.ds(pl.multiple_of(slot * 2 * rows, 2 * rows), 2 * rows)
    token[...] = jnp.zeros_like(token)
    hs[...] = rows_normalized(xa[pair, :].astype(jnp.float32), gain[...]).astype(jnp.bfloat16)
    cols = 256
    for c in range(width, 2 * width, cols):
        k = jnp.dot(hs[...], w[:, c : c + cols], preferred_element_type=jnp.float32)
        ks[slot, :, c - width : c - width + cols] = k.astype(jnp.bfloat16)
    for c in range(2 * width, 3 * width, cols):
        v = jnp.dot(hs[...], w[:, c : c + cols], preferred_element_type=jnp.float32)
        vs[slot, c - 2 * width : c - 2 * width + cols, :] = v.astype(jnp.bfloat16).T


def project(step, dy, outer, here, blocks, gain, w_qkv, previous, after, units):
    rows, width = blocks[0].shape
    rows = rows - EXTRA
    pair = 2 * rows
    pairs = units // pair
    vmem = pl.BlockSpec(memory_space=pltpu.VMEM)
    any_spec = pl.BlockSpec(memory_space=pl.ANY)
    operands = [here, *blocks, gain, w_qkv]
    in_specs = [pl.BlockSpec(memory_space=pltpu.SMEM), any_spec, any_spec, vmem, vmem]
    in_specs += [any_spec] * len(after)
    operands += list(after)
    aliases = {}
    if previous is not None:
        aliases = {len(operands) + i: i for i in range(4)}
        in_specs += [any_spec] * 4
        operands += list(previous)
    return pl.pallas_call(
        functools.partial(project_body, step, dy, outer),
        out_shape=(
            pltpu.VMEM((pairs, pair, width), jnp.bfloat16),
            pltpu.VMEM((pairs, width, pair), jnp.bfloat16),
            pltpu.VMEM((units, width), jnp.bfloat16),
            pltpu.VMEM((units // rows, EXTRA, 2 * rows), jnp.bfloat16),
            pltpu.VMEM((8, 128), jnp.float32),
        ),
        in_specs=in_specs,
        out_specs=(vmem,) * 5,
        scratch_shapes=[pltpu.VMEM((pair, width), jnp.bfloat16), pltpu.SemaphoreType.DMA((4,))],
        input_output_aliases=aliases,
        cost_estimate=pl.CostEstimate(
            flops=2 * pair * width * 2 * width,
            bytes_accessed=2 * (width * 2 * width + 4 * pair * width),
            transcendentals=0,
        ),
        compiler_params=pltpu.CompilerParams(vmem_limit_bytes=PROJECT_VMEM),
    )(*operands)


def frames_body(
    last, here, gain, conv_b, conv_gain, x0, x1, w_qkv, w_out, w_proj, conv_w, _0, _1, _2, _3, _4,
    out, keys, values, xa, meta, staged, wo, wp, cw, xw, qs, begun, bias, acc, acc_rest, tops,
    totals, turned, red, expanded, sc, lines, starts, ends, token, hs, sems, out_sems, pair_sems,
):
    width = w_out.shape[0]
    channels = w_proj.shape[1]
    head = width // HEADS
    deep = GROUP * head
    frames = out.shape[0]
    tile = keys.shape[1]
    half = KERNEL // 2
    scale = math.log2(math.e) / math.sqrt(head)

    load_o = pltpu.make_async_copy(w_out, wo, sems.at[1])
    load_p = pltpu.make_async_copy(w_proj, wp, sems.at[2])
    load_c = pltpu.make_async_copy(conv_w, cw, sems.at[3])
    load_o.start()
    load_p.start()
    load_c.start()

    project_body(
        *last, here, x0, x1, gain, w_qkv, keys, values, xa, meta, token, hs, pair_sems
    )
    plan(frames, here[0], meta, sc, lines, starts, ends)
    base, windows, frame0 = sc[0], sc[1], sc[2]

    def seg_start(v):
        return sc[4 + v]

    def window(w, carry):
        r0 = pl.multiple_of(base + w * WIN, ALIGN)
        load_x = pltpu.make_async_copy(xa.at[pl.ds(r0, WIN)], xw, sems.at[4])
        load_x.start()
        lo, hi = jnp.int32(0), jnp.int32(0)
        for v in range(SEGS):
            lo = jnp.where(r0 >= seg_start(v), seg_start(v), lo)
            hi = jnp.where(r0 + WIN - 1 >= seg_start(v), seg_start(v + 1), hi)
        t0 = lax.div(lo, tile)
        t1 = lax.div(hi + tile - 1, tile)

        load_x.wait()
        h = rows_normalized(xw[...].astype(jnp.float32), gain[...]).astype(jnp.bfloat16)
        q = jnp.dot(h, w_qkv[:, :width], preferred_element_type=jnp.float32).astype(jnp.bfloat16)
        owner = lax.broadcasted_iota(jnp.int32, (WIN, deep), 1) // head
        zero = jnp.zeros((WIN, deep), jnp.bfloat16)
        for g in range(HEADS // GROUP):
            part = q[:, g * deep : (g + 1) * deep]
            for j in range(GROUP):
                alone = jnp.where(owner == j, part, zero)
                qs[g, j * MAIN : (j + 1) * MAIN, :] = alone[:MAIN]
                start = GROUP * MAIN + j * REST
                qs[g, start : start + REST, :] = alone[MAIN:]
        acc[...] = jnp.zeros_like(acc)
        acc_rest[...] = jnp.zeros_like(acc_rest)
        tops[...] = jnp.full_like(tops, LOW)
        totals[...] = jnp.zeros_like(totals)

        lane = lax.broadcasted_iota(jnp.int32, (1, 2 * MAIN), 1)
        row = r0 + jnp.where(lane < MAIN, lane, MAIN + (lane - MAIN) % REST)
        row_lo = jnp.zeros_like(row)
        row_hi = jnp.zeros_like(row)
        for v in range(SEGS):
            row_lo = jnp.where(row >= seg_start(v), seg_start(v), row_lo)
            row_hi = jnp.where(row >= seg_start(v), seg_start(v + 1), row_hi)

        def scores(t, g):
            dims = slice(g * deep, (g + 1) * deep)
            return lax.dot_general(
                keys[t, :, dims], qs[g], (((1,), (1,)), ((), ())),
                preferred_element_type=jnp.float32,
            )

        begun[...] = scores(t0, 0)

        def key_step(t, c):
            key = t * tile + lax.broadcasted_iota(jnp.int32, (tile, 2 * MAIN), 0)
            bias[...] = jnp.where((key >= row_lo) & (key < row_hi), 0.0, MASKED)
            groups = HEADS // GROUP

            ahead = begun[...]
            for g in range(groups):
                dims = slice(g * deep, (g + 1) * deep)
                now = ahead
                if g + 1 < groups:
                    ahead = scores(t, g + 1)
                else:
                    begun[...] = scores(jnp.minimum(t + 1, t1 - 1), 0)
                for j in range(GROUP + 1):
                    lanes = slice(j * MAIN, (j + 1) * MAIN)
                    s = now[:, lanes] * scale + (bias[:, :MAIN] if j < GROUP else bias[:, MAIN:])
                    top = tops[g][:, lanes]
                    new_top = jnp.maximum(top, jnp.max(s, axis=0, keepdims=True))
                    expo = jnp.exp2(s - new_top)
                    alpha = jnp.exp2(top - new_top)
                    tops[g, :, lanes] = new_top
                    totals[g, :, lanes] = totals[g][:, lanes] * alpha + jnp.sum(expo, axis=0, keepdims=True)
                    expo = expo.astype(jnp.bfloat16)
                    if j < GROUP:
                        start = g * deep + j * head
                        acc[g, j] = acc[g, j] * alpha + jnp.dot(
                            values[t, start : start + head, :], expo, preferred_element_type=jnp.float32
                        )
                    else:
                        acc_rest[g] = acc_rest[g] * alpha + jnp.dot(
                            values[t, dims, :], expo, preferred_element_type=jnp.float32
                        )
            return c

        lax.fori_loop(t0, t1, key_step, 0)

        for g in range(HEADS // GROUP):
            total = totals[g]
            total = jnp.where(total == 0.0, 1.0, total)
            for j in range(GROUP):
                start = g * deep + j * head
                lanes = slice(j * MAIN, (j + 1) * MAIN)
                turned[start : start + head, :MAIN] = acc[g, j] / total[:, lanes]
            rest = acc_rest[g] / total[:, GROUP * MAIN :]
            for j in range(GROUP):
                start = g * deep + j * head
                turned[start : start + head, MAIN:WIN] = rest[
                    j * head : (j + 1) * head, j * REST : (j + 1) * REST
                ]
        attended = turned[...].T[:WIN].astype(jnp.bfloat16)

        @pl.when(w == 0)
        def _():
            load_o.wait()
            load_p.wait()

        mixed = jnp.dot(attended, wo[...], preferred_element_type=jnp.float32) + xw[...].astype(
            jnp.float32
        )
        reduced = jnp.dot(
            mixed.astype(jnp.bfloat16), wp[...], preferred_element_type=jnp.float32
        ).astype(jnp.bfloat16)
        red[pl.ds(0, WIN), :] = reduced
        red[pl.ds(WIN, LANES - WIN), :] = jnp.zeros((LANES - WIN, channels), jnp.bfloat16)
        shape = (frames + 2 * HALO, LANES)
        frame = frame0 - HALO + lax.broadcasted_iota(jnp.int32, shape, 0)
        lanes = starts.shape[1]
        row0 = lax.div(r0, lanes)
        shift = 3 * lanes - lax.rem(r0, lanes)

        def cut(ref):
            line = jnp.concatenate([ref[pl.ds(row0 + i, 1), :] for i in range(3)], axis=1)
            line = pltpu.roll(jnp.broadcast_to(line, (8, 3 * lanes)), shift, 1)[:1, :LANES]
            return jnp.where(lax.broadcasted_iota(jnp.int32, (1, LANES), 1) < WIN, line, 0)

        pick = jnp.where((frame >= cut(starts)) & (frame < cut(ends)), 1.0, 0.0).astype(jnp.bfloat16)
        rows = jnp.dot(pick, red[...], preferred_element_type=jnp.float32)

        @pl.when(w == 0)
        def _():
            expanded[...] = rows

        @pl.when(w > 0)
        def _():
            expanded[...] += rows

        return carry

    lax.fori_loop(0, windows, window, 0)

    load_c.wait()
    leaving = []
    block = OUT_ROWS
    for b in range(frames // block):
        conv = jnp.zeros((block, channels), jnp.float32) + conv_b[...]
        for tap in range(KERNEL):
            part = expanded[pl.ds(b * block + HALO - half + tap, block), :].astype(jnp.bfloat16)
            conv = conv + jnp.dot(part, cw[tap], preferred_element_type=jnp.float32)
        result = expanded[pl.ds(b * block + HALO, block), :] + rows_normalized(
            jnp.maximum(conv, 0.0), conv_gain[...]
        )
        part = pl.ds(b * block, block)
        staged[part, :] = result.astype(jnp.bfloat16)
        leaving.append(pltpu.make_async_copy(staged.at[part], out.at[part], out_sems.at[b]))
        leaving[-1].start()
    for copy in leaving:
        copy.wait()


def frames_call(
    last, here, gain, conv_b, conv_gain, blocks, w_qkv, w_out, w_proj, conv_w, state, token, frames
):
    ks, _, xa, meta = state
    width = xa.shape[1]
    channels = w_proj.shape[1]
    head = width // HEADS
    hbm = pl.BlockSpec(memory_space=pltpu.HBM)
    vmem = pl.BlockSpec(memory_space=pltpu.VMEM)
    any_spec = pl.BlockSpec(memory_space=pl.ANY)
    groups = HEADS // GROUP
    return pl.pallas_call(
        functools.partial(frames_body, last),
        out_shape=(
            jax.ShapeDtypeStruct((frames, channels), jnp.bfloat16),
            *[pltpu.VMEM(array.shape, array.dtype) for array in state],
        ),
        in_specs=[pl.BlockSpec(memory_space=pltpu.SMEM)]
        + [vmem] * 3 + [any_spec] * 2 + [vmem] + [hbm] * 3 + [any_spec] * 5,
        out_specs=(hbm,) + (vmem,) * 4,
        input_output_aliases={10 + i: 1 + i for i in range(4)},
        scratch_shapes=[
            pltpu.VMEM((frames, channels), jnp.bfloat16),
            pltpu.VMEM((width, width), jnp.bfloat16),
            pltpu.VMEM((width, channels), jnp.bfloat16),
            pltpu.VMEM((KERNEL, channels, channels), jnp.bfloat16),
            pltpu.VMEM((WIN, width), jnp.bfloat16),
            pltpu.VMEM((groups, STACK, GROUP * head), jnp.bfloat16),
            pltpu.VMEM((ks.shape[1], STACK), jnp.float32),
            pltpu.VMEM((ks.shape[1], 2 * MAIN), jnp.float32),
            pltpu.VMEM((groups, GROUP, head, MAIN), jnp.float32),
            pltpu.VMEM((groups, GROUP * head, GROUP * REST), jnp.float32),
            pltpu.VMEM((groups, 1, STACK), jnp.float32),
            pltpu.VMEM((groups, 1, STACK), jnp.float32),
            pltpu.VMEM((width, 2 * MAIN), jnp.float32),
            pltpu.VMEM((LANES, channels), jnp.bfloat16),
            pltpu.VMEM((frames + 2 * HALO, channels), jnp.float32),
            pltpu.SMEM((SEGS + 5,), jnp.int32),
            pltpu.VMEM((meta.shape[0], meta.shape[2]), jnp.float32),
            pltpu.VMEM((meta.shape[0] + 8, meta.shape[2] // 2), jnp.int32),
            pltpu.VMEM((meta.shape[0] + 8, meta.shape[2] // 2), jnp.int32),
            pltpu.VMEM((8, 128), jnp.float32),
            pltpu.VMEM((ks.shape[1], width), jnp.bfloat16),
            pltpu.SemaphoreType.DMA((5,)),
            pltpu.SemaphoreType.DMA((frames // OUT_ROWS,)),
            pltpu.SemaphoreType.DMA((4,)),
        ],
        compiler_params=pltpu.CompilerParams(vmem_limit_bytes=FRAMES_VMEM),
    )(here, gain, conv_b, conv_gain, *blocks, w_qkv, w_out, w_proj, conv_w, *state, token)[0]


def local(units, durations, seg_ids, ln_gain, w_qkv, w_out, w_proj, conv_w, conv_b, conv_gain):
    n = lax.axis_size("seq")
    outer = n // 4
    here = lax.axis_index("seq")
    count = units.shape[0]
    total = n * count
    frame_count = DUR_MEAN * count

    def place(z, y, c):
        return (z * 2 + y) * 2 + c

    def pairs(step, dy, dc):
        return [
            (place(z, y, c), place((z + step) % outer, y ^ dy, c ^ dc))
            for z in range(outer)
            for y in range(2)
            for c in range(2)
        ]

    def send(value, step, dy=0, dc=0):
        return lax.ppermute(value, "seq", pairs(step, dy, dc))

    gain = ln_gain[None, :]
    w_out, w_proj, conv_w = [
        pltpu.with_memory_space_constraint(w, pltpu.HBM) for w in (w_out, w_proj, conv_w)
    ]
    where = here.reshape(1)

    def kernel(distance, dy, blocks, state, *after):
        *state, token = project(
            distance % outer, dy, outer, where, blocks, gain, w_qkv, state, after, total
        )
        return state, token

    w_qkv, token = load(where, w_qkv)
    far_up, far_down = outer // 2, (outer - 1) // 2

    def in_rounds(own, state, token):
        up = down = own
        arrived = [(0, own)]
        waiting = []
        for step in range(far_up + 1):
            following = []
            if step < far_up:
                up = send(up, 1)
                following.append((step + 1, up))
            if step < far_down:
                down = send(down, outer - 1)
                following.append((-(step + 1), down))
            for pair in waiting:
                state, token = kernel(*pair, state, token)
            if waiting and following:
                held = lax.optimization_barrier((token, *[block for _, block in arrived]))
                token = held[0]
                arrived = [(d, block) for (d, _), block in zip(arrived, held[1:])]
            sides = []
            for d, block in arrived:
                if step == far_up and step > 1:
                    across = send(waiting_up, 1)
                else:
                    across = send(block, 0, 1, 0)
                sides.append((d, block, across, send(block, 0, 0, 1)))
            for d, block, across, beside in sides:
                state, token = kernel(d, 0, (block, beside), state, token)
            if step == 0:
                ((d, _, across, _),) = sides
                token, across = lax.optimization_barrier((token, across))
                diagonal = send(across, 0, 0, 1)
                state, token = kernel(d, 1, (across, diagonal), state, token)
            halves = [across for _, _, across, _ in sides]
            if following:
                held = lax.optimization_barrier((token, *[block for _, block in following]))
                token = held[0]
                following = [(d, block) for (d, _), block in zip(following, held[1:])]
                up = following[0][1]
                down = following[1][1] if len(following) > 1 else None
            waiting = []
            for (d, _, _, _), across in zip(sides if step > 0 else (), halves):
                token, across = lax.optimization_barrier((token, across))
                waiting.append((d, 1, (across, send(across, 0, 0, 1))))
            waiting_up = sides[0][2]
            arrived = following
        for pair in waiting[:-1]:
            state, token = kernel(*pair, state, token)
        return state, token, waiting[-1]

    def four_planes(own, state, token):
        def tie(token, *blocks):
            return lax.optimization_barrier((token, *blocks))

        up = send(own, 1)
        across = send(own, 0, 1, 0)
        beside = send(own, 0, 0, 1)
        token, later = tie(token, own)
        down = send(later, outer - 1)
        state, token = kernel(0, 0, (own, beside), state, token)
        token, up = tie(token, up)
        far = send(up, 1)
        up_across = send(up, 0, 1, 0)
        up_beside = send(up, 0, 0, 1)
        token, across = tie(token, across)
        diagonal = send(across, 0, 0, 1)
        state, token = kernel(1, 0, (up, up_beside), state, token)
        state, token = kernel(0, 1, (across, diagonal), state, token)
        token, down = tie(token, down)
        down_across = send(down, 0, 1, 0)
        down_beside = send(down, 0, 0, 1)
        token, up_across = tie(token, up_across)
        far_across = send(up_across, 1)
        up_diagonal = send(up_across, 0, 0, 1)
        state, token = kernel(-1, 0, (down, down_beside), state, token)
        state, token = kernel(1, 1, (up_across, up_diagonal), state, token)
        token, far = tie(token, far)
        far_beside = send(far, 0, 0, 1)
        token, down_across = tie(token, down_across)
        down_diagonal = send(down_across, 0, 0, 1)
        state, token = kernel(2, 0, (far, far_beside), state, token)
        state, token = kernel(-1, 1, (down_across, down_diagonal), state, token)
        token, far_across = tie(token, far_across)
        far_diagonal = send(far_across, 0, 0, 1)
        return state, token, (2, 1, (far_across, far_diagonal))

    own = pack(where, units, durations[None, :], seg_ids[None, :])
    run = four_planes if outer == 4 else in_rounds
    state, token, (distance, dy, blocks) = run(own, None, token)
    return frames_call(
        (distance % outer, dy, outer), where, gain, conv_b[None, :], conv_gain[None, :], blocks,
        w_qkv, w_out, w_proj, conv_w, state, token, frame_count,
    )


def solution(mesh):
    split = P(("grp", "seq"))
    in_specs = (P(("grp", "seq"), None), split, split) + (P(),) * 7
    return jax.shard_map(
        local, mesh=mesh, in_specs=in_specs, out_specs=P(("grp", "seq"), None), check_vma=False
    )
```
